32 devices in a mesh: groups: 2 (over x), seq: 16 (over z, y, core).
Axes of the slice: x: 2, y: 2, z: 4, core: 2. Of those that a mesh axis runs over, the one named last changes fastest.
Arguments:
- queries: bfloat16 [12288, 2240], P(('groups', 'seq')), parts along dimension 0, may hold values from -6 to 6
- key_rows: bfloat16 [12288, 2240], P(('groups', 'seq')), parts along dimension 0, may hold values from -6 to 6
- value_rows: bfloat16 [12288, 2240], P(('groups', 'seq')), parts along dimension 0, may hold values from -6 to 6
- frame_len: int32 [32, 2], P(('groups', 'seq')), parts along dimension 0, may hold values from 1 to 240, 384 in all within a row
- log_decay: float32 [32, 2, 20], P(('groups', 'seq')), parts along dimension 0, may hold values from -6 to 0
- timestep: int32 [32], P(('groups', 'seq')), parts along dimension 0, may hold values from 0 to 49
- conv_kernel: float32 [4, 2240], replicated, may hold values from -3 to 3
- norm_gain: float32 [2240], replicated, may hold values from 0.1 to 1.9
- mod_table: float32 [50, 2240], replicated, may hold values from -3 to 3
- out_grad: bfloat16 [12288, 2240], P(('groups', 'seq')), parts along dimension 0, may hold values from -6 to 6
Outputs:
- grad_queries: bfloat16 [12288, 2240], P(('groups', 'seq')), parts along dimension 0
- grad_keys: bfloat16 [12288, 2240], P(('groups', 'seq')), parts along dimension 0
- grad_values: bfloat16 [12288, 2240], P(('groups', 'seq')), parts along dimension 0
- grad_kernel: float32 [8, 2240], P('groups'), parts along dimension 0
- grad_gain: float32 [4480], P('groups'), parts along dimension 0
- grad_table: float32 [100, 2240], P('groups'), parts along dimension 0
The draws below stay inside these ranges and needn't reach their ends.
There are 2 independent parts, one for each index of `groups`. The reference program is written for one: setup_inputs(seed, part) draws one part's arguments, and reference() takes and returns one part's arrays. A program takes and returns all parts, laid end to end along the dimension named above; an argument that names none is the same for every part. Nothing has to cross between parts.
Inputs may be any that keep to these rules, and one draw needn't show every extreme that they name: `frame_len`: the 2 frames of each block hold 384 tokens together, and in every block the longest frame has at most 240 tokens.
All inputs are finite; a program needn't handle non-finite values.
Results may differ from the reference program's by a relative error of at most 0.0058.
Values may be sent and summed in bfloat16 or wider, within the bound.
A program may use at most 384 MiB of HBM per device.

```python
import math
import jax
import jax.numpy as jnp
import numpy as np
from jax import lax

H = 20
HD = 112
C = 2240
TOK_DEV = 384
FPD = 2
FMAX = 240
KC = 4
NT = 50
BLOCKS = 16
TOKENS = 6144


def draw_log_decay(key, part):
    random_child_keys = jax.random.split(key, 10)
    sequence_token_length = BLOCKS * FPD
    fast_count = H // 2
    cut_count = max(1, H // 10)
    head_rank = jax.random.permutation(random_child_keys[0], H)
    fast_heads = head_rank < fast_count
    early_heads = (head_rank >= fast_count) & (head_rank < fast_count + cut_count)
    late_heads = (head_rank >= fast_count + cut_count) & (head_rank < fast_count + 2 * cut_count)
    fast_rate = jnp.exp(jax.random.uniform(random_child_keys[1], (H,), minval=jnp.log(0.22), maxval=jnp.log(0.32)))
    slow_rate = jnp.exp(jax.random.uniform(random_child_keys[2], (H,), minval=jnp.log(0.1), maxval=jnp.log(0.5))) / sequence_token_length
    forgetting_rate = jnp.where(fast_heads, fast_rate, slow_rate)
    random_jitter = jax.random.uniform(random_child_keys[3], (BLOCKS, FPD, H), minval=0.8, maxval=1.6)
    spike_begin = jax.random.randint(random_child_keys[4], (2,), 0, sequence_token_length)
    spike_depth = jnp.log(jax.random.uniform(random_child_keys[5], (2,), minval=0.5, maxval=0.8))
    frame_offset = jnp.arange(sequence_token_length, dtype=jnp.int32).reshape(BLOCKS, FPD)
    spike_groups = jnp.sum(jnp.where(frame_offset[:, :, None] == spike_begin[None, None, :], spike_depth[None, None, :], 0.0), axis=2)
    early_block = BLOCKS // 16 + jax.random.randint(random_child_keys[6], (), 0, max(1, BLOCKS // 16))
    late_block = BLOCKS - 2 - jax.random.randint(random_child_keys[7], (), 0, 2)
    early_depth = jnp.log(jax.random.uniform(random_child_keys[8], (H,), minval=0.03, maxval=0.095))
    late_depth = jnp.log(jax.random.uniform(random_child_keys[9], (H,), minval=0.006, maxval=0.0095))
    early_drop = jnp.where(early_heads, early_depth, 0.0)
    late_drop = jnp.where(late_heads, late_depth, 0.0)
    early_here = (frame_offset == early_block * FPD)[:, :, None]
    late_here = (frame_offset == late_block * FPD)[:, :, None]
    split_groups = jnp.where(early_here, early_drop[None, None, :], 0.0) + jnp.where(late_here, late_drop[None, None, :], 0.0)
    computed_output = -forgetting_rate[None, None, :] * random_jitter + spike_groups[:, :, None] + split_groups
    return jnp.maximum(computed_output, -6.0).astype(jnp.float32)


def plant(array, stream_key, smallest, largest):
    place = [jax.random.randint(jax.random.fold_in(stream_key, axis), (), 0, length) for axis, length in enumerate(array.shape)]
    longest = array.shape.index(max(array.shape))
    neighbour = place[:longest] + [(place[longest] + 1) % array.shape[longest]] + place[longest + 1:]
    return array.at[tuple(place)].set(smallest).at[tuple(neighbour)].set(largest)


def level_of(own_key, shape, cuts, low, high):
    def one(dim, shards_of):
        steps = jax.random.uniform(jax.random.fold_in(jax.random.fold_in(own_key, 6), dim), (shards_of,), jnp.float32, low / len(cuts), high / len(cuts))
        return jnp.repeat(jnp.exp(steps), shape[dim] // shards_of).reshape((-1,) + (1,) * (len(shape) - dim - 1))

    level = one(*cuts[0])
    for cut in cuts[1:]:
        level = level * one(*cut)
    return level


def split_up(amount, total, most, slope):
    portions = [(1 << 20) // math.isqrt(grade ** slope) + 1 for grade in range(2, amount + 1)]
    spare, given = total - most - (amount - 1), [1] * (amount - 1)
    while spare > 0:
        free = [i for i in range(amount - 1) if given[i] < most]
        mass, budget = sum([portions[i] for i in free]), spare
        for i in free:
            more = min(most - given[i], max(1, budget * portions[i] // mass), spare)
            given[i] = given[i] + more
            spare = spare - more
    return np.array([most] + given)


def ragged(own_key, number_of, total, limit, lean):
    if number_of == 2:
        one = jax.random.randint(own_key, (), max(1, total - limit), min(limit, total - 1) + 1)
        return jnp.stack([one, total - one])
    sizes = jnp.asarray(split_up(number_of, total, limit, lean), jnp.int32)
    couples = (number_of - 1) // 2
    source_of, receiver = sizes[1:1 + 2 * couples:2], sizes[2:2 + 2 * couples:2]
    margin = jnp.minimum(source_of - 1, limit - receiver)
    passed = jax.random.randint(jax.random.fold_in(own_key, 1), (couples,), 0, 1 << 20) % (margin + 1)
    sizes = sizes.at[1:1 + 2 * couples:2].set(source_of - passed).at[2:2 + 2 * couples:2].set(receiver + passed)
    return sizes[jax.random.permutation(jax.random.fold_in(own_key, 2), number_of)]


def gaussian(key, shape, scale, bound, cuts=(), held_as=jnp.bfloat16):
    drawn = jax.random.normal(key, shape, jnp.float32) * scale
    if len(cuts) > 0:
        drawn = level_of(key, shape, cuts, -0.22, 0.18) * drawn
    return jnp.clip(drawn, min=-bound, max=bound).astype(held_as)


def setup_inputs(seed: int = 0, part: int = 0) -> dict:
    streams_of = jax.random.split(jax.random.key(seed), 11)
    own_keys = jax.random.split(jax.random.fold_in(streams_of[10], part), 11)
    queries = gaussian(own_keys[0], (TOKENS, C), 1.0, 6.0, ((0, 16),))
    key_rows = gaussian(own_keys[1], (TOKENS, C), 1.0, 6.0, ((0, 16),))
    value_rows = gaussian(own_keys[2], (TOKENS, C), 1.0, 6.0, ((0, 16),))
    frame_len = jax.vmap(lambda own: ragged(own, FPD, TOK_DEV, FMAX, 1))(jax.random.split(own_keys[3], BLOCKS)).reshape((BLOCKS, FPD)).astype(jnp.int32)
    log_decay = draw_log_decay(jax.random.fold_in(jax.random.fold_in(streams_of[10], part), 71), part)
    timestep = plant(jax.random.randint(own_keys[5], (BLOCKS,), 0, NT), jax.random.fold_in(own_keys[5], 1), 0, NT - 1).astype(jnp.int32)
    conv_kernel = gaussian(streams_of[6], (KC, C), 0.5, 3.0, (), jnp.float32)
    norm_gain = jnp.clip(1.0 + 0.18 * jax.random.normal(streams_of[7], (C,), jnp.float32), 0.1, 1.9)
    mod_table = gaussian(streams_of[8], (NT, C), 0.5, 3.0, (), jnp.float32)
    out_grad = gaussian(own_keys[9], (TOKENS, C), 1.0, 6.0, ((0, 16),))
    return {"queries": queries, "key_rows": key_rows, "value_rows": value_rows, "frame_len": frame_len, "log_decay": log_decay, "timestep": timestep, "conv_kernel": conv_kernel, "norm_gain": norm_gain, "mod_table": mod_table, "out_grad": out_grad}


EPSILON = 1e-06

def frame_layout(lengths, decays, count):
    bounds = jnp.cumsum(lengths).astype(jnp.int32)
    position = jnp.arange(count, dtype=jnp.int32)
    frame_id = lax.optimization_barrier(jnp.sum((position[:, None] >= bounds[None, :]).astype(jnp.int32), axis=1))
    frame_cum = jnp.cumsum(decays, axis=0)
    frame_numbers = jnp.arange(lengths.shape[0], dtype=jnp.int32)
    selector = (frame_id[:, None] == frame_numbers[None, :]).astype(decays.dtype)
    token_decay = lax.optimization_barrier(jnp.sum(selector[:, :, None] * frame_cum[None, :, :], axis=1))
    return (frame_id, token_decay, frame_cum[-1])

def decay_weights(frame_id, token_decay):
    allowed = (frame_id[:, None] >= frame_id[None, :])[None, :, :]
    head_major = token_decay.T
    spread = head_major[:, :, None] - head_major[:, None, :]
    return jnp.where(allowed, jnp.exp(jnp.where(allowed, spread, 0.0)), 0.0)

def causal_conv(padded, kernel, count):
    tap_count = kernel.shape[0]
    computed_output = jnp.zeros((count, kernel.shape[1]), jnp.float32)
    for offset in range(tap_count):
        computed_output = computed_output + kernel[offset] * padded[tap_count - 1 - offset:tap_count - 1 - offset + count]
    return computed_output

def conv_back(padded_grad, kernel, count):
    computed_output = jnp.zeros((count, kernel.shape[1]), jnp.float32)
    for offset in range(kernel.shape[0]):
        computed_output = computed_output + kernel[offset] * padded_grad[offset:offset + count]
    return computed_output

def reference(queries, key_rows, value_rows, frame_len, log_decay, timestep, conv_kernel, norm_gain, mod_table, out_grad):
    score_scale = HD ** (-0.5)
    exact = lax.Precision.HIGHEST
    padded = jnp.concatenate([jnp.zeros((KC - 1, C), jnp.float32), value_rows.astype(jnp.float32)], axis=0)
    conv_values = causal_conv(padded, conv_kernel, TOKENS).astype(jnp.bfloat16)
    query_blocks = queries.reshape(BLOCKS, TOK_DEV, H, HD)
    key_blocks = key_rows.reshape(BLOCKS, TOK_DEV, H, HD)
    value_blocks = conv_values.reshape(BLOCKS, TOK_DEV, H, HD)
    grad_blocks = out_grad.reshape(BLOCKS, TOK_DEV, H, HD)
    mod_rows = mod_table[timestep]

    def forward_step(state, pieces):
        key_block, value_block, lengths, decays = pieces
        frame_id, token_decay, block_decay = frame_layout(lengths, decays, TOK_DEV)
        into_end = jnp.exp(block_decay[None, :] - token_decay)
        scaled_keys = key_block.astype(jnp.float32) * into_end[:, :, None]
        local_state = jnp.einsum('thd,the->hde', scaled_keys, value_block.astype(jnp.float32), precision=exact)
        return (jnp.exp(block_decay)[:, None, None] * state + local_state, state)
    zero_state = jnp.zeros((H, HD, HD), jnp.float32)
    final_state, states_in = lax.scan(forward_step, zero_state, (key_blocks, value_blocks, frame_len, log_decay))

    def first_pass(pieces):
        query_block, key_block, value_block, lengths, decays, state_in, grad_block, mod_row = pieces
        frame_id, token_decay, block_decay = frame_layout(lengths, decays, TOK_DEV)
        weights_mask = decay_weights(frame_id, token_decay)
        from_start = jnp.exp(token_decay)
        query_float = query_block.astype(jnp.float32)
        key_float = key_block.astype(jnp.float32)
        value_float = value_block.astype(jnp.float32)
        scores = jnp.einsum('thd,shd->hts', query_float, key_float)
        attn_weights = (scores * weights_mask * score_scale).astype(jnp.bfloat16)
        numerator = jnp.einsum('hts,shd->thd', attn_weights.astype(jnp.float32), value_float)
        scaled_queries = query_float * (score_scale * from_start)[:, :, None]
        numerator = numerator + jnp.einsum('thd,hde->the', scaled_queries, state_in, precision=exact)
        inv_rms = lax.rsqrt(lax.optimization_barrier(jnp.mean(numerator * numerator, axis=2, keepdims=True)) + EPSILON)
        normed = numerator * inv_rms
        upstream = grad_block.astype(jnp.float32)
        normed_grad = upstream * (norm_gain * (1.0 + mod_row)).reshape(H, HD)
        numer_grad = inv_rms * (normed_grad - normed * lax.optimization_barrier(jnp.mean(normed_grad * normed, axis=2, keepdims=True)))
        grad_rounded = numer_grad.astype(jnp.bfloat16)
        rounded_float = grad_rounded.astype(jnp.float32)
        score_grad = jnp.einsum('thd,shd->hts', rounded_float, value_float)
        score_grad = (score_grad * weights_mask * score_scale).astype(jnp.bfloat16).astype(jnp.float32)
        adjoint_local = jnp.einsum('thd,the->hde', scaled_queries, numer_grad, precision=exact)
        query_grad = jnp.einsum('hts,shd->thd', score_grad, key_float)
        query_grad = query_grad + (score_scale * from_start)[:, :, None] * jnp.einsum('the,hde->thd', numer_grad, state_in, precision=exact)
        key_local = jnp.einsum('hts,thd->shd', score_grad, query_float)
        value_local = jnp.einsum('hts,thd->shd', attn_weights.astype(jnp.float32), rounded_float)
        block_terms = lax.optimization_barrier(jnp.sum((upstream * normed).reshape(TOK_DEV, C), axis=0))
        return (query_grad.astype(jnp.bfloat16), key_local, value_local, adjoint_local, block_terms, jnp.exp(block_decay))
    first = lax.map(first_pass, (query_blocks, key_blocks, value_blocks, frame_len, log_decay, states_in, grad_blocks, mod_rows))
    query_grads, key_locals, value_locals, adjoint_locals, block_terms, block_factors = first

    def backward_step(running, pieces):
        factor, local_part = pieces
        return (factor[:, None, None] * running + local_part, running)
    last_adjoint, adjoints = lax.scan(backward_step, zero_state, (block_factors, adjoint_locals), reverse=True)

    def second_pass(pieces):
        key_block, value_block, lengths, decays, adjoint, key_local, value_local = pieces
        frame_id, token_decay, block_decay = frame_layout(lengths, decays, TOK_DEV)
        into_end = jnp.exp(block_decay[None, :] - token_decay)
        scaled_keys = key_block.astype(jnp.float32) * into_end[:, :, None]
        key_grad = key_local + into_end[:, :, None] * jnp.einsum('the,hde->thd', value_block.astype(jnp.float32), adjoint, precision=exact)
        value_grad = value_local + jnp.einsum('thd,hde->the', scaled_keys, adjoint, precision=exact)
        return (key_grad.astype(jnp.bfloat16), value_grad)
    key_grads, value_grads = lax.map(second_pass, (key_blocks, value_blocks, frame_len, log_decay, adjoints, key_locals, value_locals))
    conv_grad = value_grads.reshape(TOKENS, C)
    padded_grad = jnp.concatenate([conv_grad, jnp.zeros((KC - 1, C), jnp.float32)], axis=0)
    grad_values = conv_back(padded_grad, conv_kernel, TOKENS).astype(jnp.bfloat16)
    kernel_rows = [lax.optimization_barrier(jnp.sum(conv_grad * padded[KC - 1 - offset:KC - 1 - offset + TOKENS], axis=0)) for offset in range(KC)]
    grad_kernel = jnp.stack(kernel_rows, axis=0) / BLOCKS
    grad_gain = lax.optimization_barrier(jnp.sum(block_terms * (1.0 + mod_rows), axis=0)) / BLOCKS
    selector = (timestep[:, None] == jnp.arange(NT, dtype=jnp.int32)[None, :]).astype(jnp.float32)
    grad_table = jnp.dot(selector.T, block_terms * norm_gain, precision=exact) / BLOCKS
    return (query_grads.reshape(TOKENS, C), key_grads.reshape(TOKENS, C), grad_values, grad_kernel, grad_gain, grad_table)
```

```python
import functools

import jax
import jax.numpy as jnp
from jax import lax
from jax.experimental import pallas as pl
from jax.experimental.pallas import tpu as pltpu
from jax.sharding import PartitionSpec as P

EPSILON = 1e-06
MESH = pl.DeviceIdType.MESH


def scan_kernel(n, rows, head_dim, reverse, *refs):
    if reverse:
        (pieces, extra, decays, out, extra_all, inbox, outbox) = refs[:7]
    else:
        (pieces, extra, out, extra_all, inbox, outbox) = refs[:6]
        decays = extra_all
    (in_send, in_recv, ex_send, ex_recv, out_send, out_recv) = refs[-6:]
    me = lax.axis_index("seq")
    group = lax.axis_index("groups")

    def where(peer):
        return (group, peer)

    def piece_copy(peer, slot):
        return pltpu.make_async_remote_copy(
            src_ref=pieces.at[peer], dst_ref=inbox.at[slot],
            send_sem=in_send.at[peer], recv_sem=in_recv.at[slot],
            device_id=where(peer), device_id_type=MESH)

    def extra_copy(peer, slot):
        return pltpu.make_async_remote_copy(
            src_ref=extra, dst_ref=extra_all.at[slot],
            send_sem=ex_send.at[peer], recv_sem=ex_recv.at[slot],
            device_id=where(peer), device_id_type=MESH)

    def result_copy(peer, slot):
        return pltpu.make_async_remote_copy(
            src_ref=outbox.at[peer], dst_ref=out.at[slot],
            send_sem=out_send.at[peer], recv_sem=out_recv.at[slot],
            device_id=where(peer), device_id_type=MESH)

    barrier = pltpu.get_barrier_semaphore()

    def greet(k, c):
        pl.semaphore_signal(barrier, inc=1, device_id=where(lax.rem(me + k, n)), device_id_type=MESH)
        return c

    lax.fori_loop(1, n, greet, 0)
    inbox[me] = pieces[me]
    extra_all[me] = extra[...]
    pl.semaphore_wait(barrier, n - 1)

    def send(k, c):
        peer = lax.rem(me + k, n)
        extra_copy(peer, me).start()
        piece_copy(peer, me).start()
        return c

    lax.fori_loop(1, n, send, 0)

    lane = lax.broadcasted_iota(jnp.int32, (rows, 128), 1) * head_dim
    index = lax.broadcasted_iota(jnp.int32, (rows, 128), 0) + me * rows
    mine = (index >= lane) & (index < lane + head_dim)

    def step(i, state):
        b = n - 1 - i if reverse else i

        @pl.when(b != me)
        def _():
            extra_copy(b, b).wait_recv()
            piece_copy(b, b).wait_recv()

        outbox[b] = state.astype(jnp.bfloat16)

        @pl.when(b != me)
        def _():
            result_copy(b, me).start()

        row = decays[b]
        factor = jnp.exp(jnp.sum(jnp.where(mine, row, 0.0), axis=1, keepdims=True))
        return factor * state + inbox[b].astype(jnp.float32)

    lax.fori_loop(0, n, step, jnp.zeros(inbox.shape[1:], jnp.float32))
    out[me] = outbox[me]

    def finish(k, c):
        peer = lax.rem(me + k, n)
        extra_copy(peer, peer).wait_send()
        piece_copy(peer, peer).wait_send()
        result_copy(peer, peer).wait_send()
        result_copy(peer, peer).wait_recv()
        return c

    lax.fori_loop(1, n, finish, 0)


def carried(state, extra, decays, reverse):
    n = lax.axis_size("seq")
    heads, depth, width = state.shape
    total = heads * depth
    rows = -(-total // (16 * n)) * 16
    flat = jnp.pad(state.reshape(total, width), ((0, n * rows - total), (0, 0)))
    pieces = flat.reshape(n, rows, width)
    vmem = pl.BlockSpec(memory_space=pltpu.VMEM)
    args = (pieces, extra) + ((decays,) if reverse else ())
    out, gathered = pl.pallas_call(
        functools.partial(scan_kernel, n, rows, depth, reverse),
        out_shape=(
            jax.ShapeDtypeStruct((n, rows, width), jnp.bfloat16),
            jax.ShapeDtypeStruct((n,) + extra.shape, jnp.float32),
        ),
        in_specs=[vmem] * len(args),
        out_specs=(vmem, vmem),
        scratch_shapes=[pltpu.VMEM((n, rows, width), jnp.bfloat16)] * 2
        + [pltpu.SemaphoreType.DMA((n,))] * 6,
        compiler_params=pltpu.CompilerParams(
            collective_id=1 if reverse else 0, has_side_effects=True, vmem_limit_bytes=48 << 20),
        name="adjoint_scan" if reverse else "state_scan",
    )(*args)
    return out.reshape(n * rows, width)[:total].reshape(heads, depth, width), gathered


def tail_kernel(n, terms, edge, total, following, held, landed, send_sem, recv_sem, edge_send, edge_recv):
    me = lax.axis_index("seq")
    group = lax.axis_index("groups")
    steps = n.bit_length() - 1
    barrier = pltpu.get_barrier_semaphore()
    partners = [me + (1 << i) - (2 << i) * ((me // (1 << i)) % 2) for i in range(steps)]
    for partner in partners:
        pl.semaphore_signal(barrier, inc=1, device_id=(group, partner), device_id_type=MESH)
    before, after = lax.rem(me + n - 1, n), lax.rem(me + 1, n)
    for peer in (before, after):
        pl.semaphore_signal(barrier, inc=1, device_id=(group, peer), device_id_type=MESH)
    pl.semaphore_wait(barrier, steps + 2)
    edge_copy = pltpu.make_async_remote_copy(
        src_ref=edge, dst_ref=following, send_sem=edge_send, recv_sem=edge_recv,
        device_id=(group, before), device_id_type=MESH)
    edge_copy.start()
    held[0] = terms[...]
    for i, partner in enumerate(partners):
        copy = pltpu.make_async_remote_copy(
            src_ref=held.at[i], dst_ref=landed.at[i], send_sem=send_sem.at[i], recv_sem=recv_sem.at[i],
            device_id=(group, partner), device_id_type=MESH)
        copy.start()
        copy.wait()
        held[i + 1] = held[i] + landed[i]
    total[...] = held[steps]
    edge_copy.wait()


def tail_exchange(terms, edge):
    n = lax.axis_size("seq")
    steps = n.bit_length() - 1
    vmem = pl.BlockSpec(memory_space=pltpu.VMEM)
    return pl.pallas_call(
        functools.partial(tail_kernel, n),
        out_shape=(jax.ShapeDtypeStruct(terms.shape, jnp.float32), jax.ShapeDtypeStruct(edge.shape, jnp.float32)),
        in_specs=[vmem, vmem],
        out_specs=(vmem, vmem),
        scratch_shapes=[
            pltpu.VMEM((steps + 1,) + terms.shape, jnp.float32),
            pltpu.VMEM((steps,) + terms.shape, jnp.float32),
            pltpu.SemaphoreType.DMA((steps,)),
            pltpu.SemaphoreType.DMA((steps,)),
            pltpu.SemaphoreType.DMA,
            pltpu.SemaphoreType.DMA,
        ],
        compiler_params=pltpu.CompilerParams(collective_id=2, has_side_effects=True),
        name="tail_exchange",
    )(terms, edge)


def passed_along(value, axis):
    count = lax.axis_size(axis)
    return lax.ppermute(value, axis, [(s, s + 1) for s in range(count - 1)])


def frame_layout(lengths, decays, count):
    bounds = jnp.cumsum(lengths)
    position = jnp.arange(count, dtype=jnp.int32)
    frame_id = jnp.sum((position[:, None] >= bounds[None, :]).astype(jnp.int32), axis=1)
    frame_cum = jnp.cumsum(decays, axis=0)
    frame_numbers = jnp.arange(lengths.shape[0], dtype=jnp.int32)
    selector = (frame_id[:, None] == frame_numbers[None, :]).astype(jnp.float32)
    token_decay = jnp.sum(selector[:, :, None] * frame_cum[None, :, :], axis=1)
    return (frame_id, token_decay, frame_cum)


def decay_weights(frame_id, token_decay):
    allowed = (frame_id[:, None] >= frame_id[None, :])[None, :, :]
    head_major = token_decay.T
    spread = head_major[:, :, None] - head_major[:, None, :]
    return jnp.where(allowed, jnp.exp(jnp.where(allowed, spread, 0.0)), 0.0)


def causal_conv(padded, kernel, count):
    tap_count = kernel.shape[0]
    computed_output = jnp.zeros((count, kernel.shape[1]), jnp.float32)
    for offset in range(tap_count):
        computed_output = (
            computed_output
            + kernel[offset] * padded[tap_count - 1 - offset : tap_count - 1 - offset + count]
        )
    return computed_output


def conv_back(padded_grad, kernel, count):
    computed_output = jnp.zeros((count, kernel.shape[1]), jnp.float32)
    for offset in range(kernel.shape[0]):
        computed_output = computed_output + kernel[offset] * padded_grad[offset : offset + count]
    return computed_output


def framed_outer(left, right, frame_id, weights):
    result = 0.0
    for f in range(weights.shape[0]):
        part = jnp.where((frame_id == f)[:, None, None], left, jnp.zeros_like(left))
        result = result + weights[f][:, None, None] * jnp.einsum(
            "thd,the->hde", part, right, preferred_element_type=jnp.float32)
    return result.astype(jnp.bfloat16)


def body(
    queries,
    key_rows,
    value_rows,
    frame_len,
    log_decay,
    timestep,
    conv_kernel,
    norm_gain,
    mod_table,
    out_grad,
):
    f32 = jnp.float32
    row_count, channels = queries.shape
    head_count = log_decay.shape[2]
    head_dim = channels // head_count
    score_scale = head_dim ** (-0.5)
    tap_count = conv_kernel.shape[0]
    block_count = lax.axis_size("seq")
    place = lax.axis_index("seq")
    frame_id, token_decay, frame_cum = frame_layout(frame_len[0], log_decay[0], row_count)
    block_decay = frame_cum[-1]
    previous = passed_along(value_rows[row_count - (tap_count - 1) :], "seq")
    padded = jnp.concatenate([previous, value_rows], axis=0).astype(f32)
    conv_values = causal_conv(padded, conv_kernel, row_count).astype(jnp.bfloat16)
    query_heads = queries.reshape(row_count, head_count, head_dim)
    key_heads = key_rows.reshape(row_count, head_count, head_dim)
    value_heads = conv_values.reshape(row_count, head_count, head_dim)
    into_end = jnp.exp(block_decay[None, :] - token_decay)
    from_start = jnp.exp(token_decay)
    local_state = framed_outer(key_heads, value_heads, frame_id, jnp.exp(block_decay[None, :] - frame_cum))
    lanes = jnp.concatenate([
        block_decay, timestep.astype(f32), jnp.zeros((128 - head_count - 1,), f32)])[None, :]
    state_in, gathered = carried(local_state, lanes, None, False)
    weights_mask = decay_weights(frame_id, token_decay)
    scores = jnp.einsum("thd,shd->hts", query_heads, key_heads, preferred_element_type=f32)
    attn_weights = (scores * weights_mask * score_scale).astype(jnp.bfloat16)
    numerator = jnp.einsum("hts,shd->thd", attn_weights, value_heads, preferred_element_type=f32)
    row_scale = (score_scale * from_start)[:, :, None]
    numerator = numerator + row_scale * jnp.einsum(
        "thd,hde->the", query_heads, state_in, preferred_element_type=f32)
    inv_rms = lax.rsqrt(jnp.mean(numerator * numerator, axis=2, keepdims=True) + EPSILON)
    normed = numerator * inv_rms
    levels = jnp.arange(mod_table.shape[0], dtype=jnp.int32)
    selector = (timestep[0] == levels).astype(f32)
    mod_row = jnp.sum(selector[:, None] * mod_table, axis=0)
    upstream = out_grad.astype(f32).reshape(row_count, head_count, head_dim)
    normed_grad = upstream * (norm_gain * (1.0 + mod_row)).reshape(head_count, head_dim)
    numer_grad = inv_rms * (
        normed_grad - normed * jnp.mean(normed_grad * normed, axis=2, keepdims=True)
    )
    grad_rounded = numer_grad.astype(jnp.bfloat16)
    block_terms = jnp.sum((upstream * normed).reshape(row_count, channels), axis=0)
    adjoint_local = framed_outer(query_heads, grad_rounded, frame_id, score_scale * jnp.exp(frame_cum))
    adjoint, terms_all = carried(adjoint_local, block_terms[None, :], gathered, True)
    score_grad = jnp.einsum("thd,shd->hts", grad_rounded, value_heads, preferred_element_type=f32)
    score_grad = (score_grad * weights_mask * score_scale).astype(jnp.bfloat16)
    query_grad = jnp.einsum("hts,shd->thd", score_grad, key_heads, preferred_element_type=f32)
    query_grad = query_grad + row_scale * jnp.einsum(
        "the,hde->thd", grad_rounded, state_in, preferred_element_type=f32)
    key_grad = jnp.einsum("hts,thd->shd", score_grad, query_heads, preferred_element_type=f32)
    key_grad = key_grad + into_end[:, :, None] * jnp.einsum(
        "the,hde->thd", value_heads, adjoint, preferred_element_type=f32)
    value_grad = jnp.einsum("hts,thd->shd", attn_weights, grad_rounded, preferred_element_type=f32)
    value_grad = value_grad + into_end[:, :, None] * jnp.einsum(
        "thd,hde->the", key_heads, adjoint, preferred_element_type=f32)
    conv_grad = value_grad.reshape(row_count, channels)
    kernel_terms = jnp.stack(
        [
            jnp.sum(
                conv_grad * padded[tap_count - 1 - offset : tap_count - 1 - offset + row_count],
                axis=0,
            )
            for offset in range(tap_count)
        ],
        axis=0,
    )
    kernel_sum, following = tail_exchange(kernel_terms, conv_grad[: tap_count - 1])
    following = jnp.where(place == block_count - 1, 0.0, following)
    padded_grad = jnp.concatenate([conv_grad, following], axis=0)
    input_grad = conv_back(padded_grad, conv_kernel, row_count)
    terms = terms_all[:, 0, :]
    chosen = (gathered[:, 0, head_count].astype(jnp.int32)[:, None] == levels[None, :]).astype(f32)
    sums = jnp.einsum("bl,bc->lc", chosen, terms, precision=lax.Precision.HIGHEST)
    gain_sum = jnp.sum(sums * (1.0 + mod_table), axis=0)
    table_sum = sums * norm_gain
    return (
        query_grad.reshape(row_count, channels).astype(jnp.bfloat16),
        key_grad.reshape(row_count, channels).astype(jnp.bfloat16),
        input_grad.astype(jnp.bfloat16),
        kernel_sum / block_count,
        gain_sum / block_count,
        table_sum / block_count,
    )


def solution(mesh):
    in_specs = (
        P(("groups", "seq"), None),
        P(("groups", "seq"), None),
        P(("groups", "seq"), None),
        P(("groups", "seq"), None),
        P(("groups", "seq"), None, None),
        P(("groups", "seq")),
        P(),
        P(),
        P(),
        P(("groups", "seq"), None),
    )
    out_specs = (
        P(("groups", "seq"), None),
        P(("groups", "seq"), None),
        P(("groups", "seq"), None),
        P("groups", None),
        P("groups"),
        P("groups", None),
    )
    return jax.shard_map(body, mesh=mesh, in_specs=in_specs, out_specs=out_specs, check_vma=False)
```

```python
import functools

import jax
import jax.numpy as jnp
from jax import lax
from jax.experimental import pallas as pl
from jax.experimental.pallas import tpu as pltpu
from jax.sharding import PartitionSpec as P

EPSILON = 1e-06
MESH = pl.DeviceIdType.MESH


def scan_kernel(n, rows, head_dim, reverse, *refs):
    if reverse:
        (pieces, extra, decays, out, extra_all, inbox, outbox) = refs[:7]
    else:
        (pieces, extra, out, extra_all, inbox, outbox) = refs[:6]
        decays = extra_all
    (in_send, in_recv, ex_send, ex_recv, out_send, out_recv) = refs[-6:]
    me = lax.axis_index("seq")
    group = lax.axis_index("groups")

    def where(peer):
        return (group, peer)

    def piece_copy(peer, slot):
        return pltpu.make_async_remote_copy(
            src_ref=pieces.at[peer], dst_ref=inbox.at[slot],
            send_sem=in_send.at[peer], recv_sem=in_recv.at[slot],
            device_id=where(peer), device_id_type=MESH)

    def extra_copy(peer, slot):
        return pltpu.make_async_remote_copy(
            src_ref=extra, dst_ref=extra_all.at[slot],
            send_sem=ex_send.at[peer], recv_sem=ex_recv.at[slot],
            device_id=where(peer), device_id_type=MESH)

    def result_copy(peer, slot):
        return pltpu.make_async_remote_copy(
            src_ref=outbox.at[peer], dst_ref=out.at[slot],
            send_sem=out_send.at[peer], recv_sem=out_recv.at[slot],
            device_id=where(peer), device_id_type=MESH)

    barrier = pltpu.get_barrier_semaphore()

    def greet(k, c):
        pl.semaphore_signal(barrier, inc=1, device_id=where(lax.rem(me + k, n)), device_id_type=MESH)
        return c

    lax.fori_loop(1, n, greet, 0)
    inbox[me] = pieces[me]
    extra_all[me] = extra[...]
    pl.semaphore_wait(barrier, n - 1)

    def send(k, c):
        peer = lax.rem(me + k, n)
        extra_copy(peer, me).start()
        piece_copy(peer, me).start()
        return c

    lax.fori_loop(1, n, send, 0)

    lane = lax.broadcasted_iota(jnp.int32, (rows, 128), 1) * head_dim
    index = lax.broadcasted_iota(jnp.int32, (rows, 128), 0) + me * rows
    mine = (index >= lane) & (index < lane + head_dim)

    def step(i, state):
        b = n - 1 - i if reverse else i

        @pl.when(b != me)
        def _():
            extra_copy(b, b).wait_recv()
            piece_copy(b, b).wait_recv()

        outbox[b] = state.astype(jnp.bfloat16)

        @pl.when(b != me)
        def _():
            result_copy(b, me).start()

        row = decays[b]
        factor = jnp.exp(jnp.sum(jnp.where(mine, row, 0.0), axis=1, keepdims=True))
        return factor * state + inbox[b].astype(jnp.float32)

    lax.fori_loop(0, n, step, jnp.zeros(inbox.shape[1:], jnp.float32))
    out[me] = outbox[me]

    def finish(k, c):
        peer = lax.rem(me + k, n)
        extra_copy(peer, peer).wait_send()
        piece_copy(peer, peer).wait_send()
        result_copy(peer, peer).wait_send()
        result_copy(peer, peer).wait_recv()
        return c

    lax.fori_loop(1, n, finish, 0)


def carried(flat, extra, decays, depth, reverse):
    n = lax.axis_size("seq")
    rows, width = flat.shape[0] // n, flat.shape[1]
    pieces = flat.reshape(n, rows, width)
    vmem = pl.BlockSpec(memory_space=pltpu.VMEM)
    args = (pieces, extra) + ((decays,) if reverse else ())
    out, gathered = pl.pallas_call(
        functools.partial(scan_kernel, n, rows, depth, reverse),
        out_shape=(
            jax.ShapeDtypeStruct((n, rows, width), jnp.bfloat16),
            jax.ShapeDtypeStruct((n,) + extra.shape, jnp.float32),
        ),
        in_specs=[vmem] * len(args),
        out_specs=(vmem, vmem),
        scratch_shapes=[pltpu.VMEM((n, rows, width), jnp.bfloat16)] * 2
        + [pltpu.SemaphoreType.DMA((n,))] * 6,
        compiler_params=pltpu.CompilerParams(
            collective_id=1 if reverse else 0, has_side_effects=True, vmem_limit_bytes=48 << 20),
        name="adjoint_scan" if reverse else "state_scan",
    )(*args)
    return out.reshape(n * rows, width), gathered


def tail_kernel(n, terms, edge, total, following, held, landed, send_sem, recv_sem, edge_send, edge_recv):
    me = lax.axis_index("seq")
    group = lax.axis_index("groups")
    steps = n.bit_length() - 1
    barrier = pltpu.get_barrier_semaphore()
    partners = [me + (1 << i) - (2 << i) * ((me // (1 << i)) % 2) for i in range(steps)]
    for partner in partners:
        pl.semaphore_signal(barrier, inc=1, device_id=(group, partner), device_id_type=MESH)
    before, after = lax.rem(me + n - 1, n), lax.rem(me + 1, n)
    for peer in (before, after):
        pl.semaphore_signal(barrier, inc=1, device_id=(group, peer), device_id_type=MESH)
    pl.semaphore_wait(barrier, steps + 2)
    edge_copy = pltpu.make_async_remote_copy(
        src_ref=edge, dst_ref=following, send_sem=edge_send, recv_sem=edge_recv,
        device_id=(group, before), device_id_type=MESH)
    edge_copy.start()
    held[0] = terms[...]
    for i, partner in enumerate(partners):
        copy = pltpu.make_async_remote_copy(
            src_ref=held.at[i], dst_ref=landed.at[i], send_sem=send_sem.at[i], recv_sem=recv_sem.at[i],
            device_id=(group, partner), device_id_type=MESH)
        copy.start()
        copy.wait()
        held[i + 1] = held[i] + landed[i]
    total[...] = held[steps]
    edge_copy.wait()


def tail_exchange(terms, edge):
    n = lax.axis_size("seq")
    steps = n.bit_length() - 1
    vmem = pl.BlockSpec(memory_space=pltpu.VMEM)
    return pl.pallas_call(
        functools.partial(tail_kernel, n),
        out_shape=(jax.ShapeDtypeStruct(terms.shape, jnp.float32), jax.ShapeDtypeStruct(edge.shape, jnp.float32)),
        in_specs=[vmem, vmem],
        out_specs=(vmem, vmem),
        scratch_shapes=[
            pltpu.VMEM((steps + 1,) + terms.shape, jnp.float32),
            pltpu.VMEM((steps,) + terms.shape, jnp.float32),
            pltpu.SemaphoreType.DMA((steps,)),
            pltpu.SemaphoreType.DMA((steps,)),
            pltpu.SemaphoreType.DMA,
            pltpu.SemaphoreType.DMA,
        ],
        compiler_params=pltpu.CompilerParams(collective_id=2, has_side_effects=True),
        name="tail_exchange",
    )(terms, edge)


def passed_along(value, axis):
    count = lax.axis_size(axis)
    return lax.ppermute(value, axis, [(s, s + 1) for s in range(count - 1)])


def chunks(width, size):
    return [slice(c, min(c + size, width)) for c in range(0, width, size)]


def mm(a, b, ca, cb):
    return lax.dot_general(a, b, (((ca,), (cb,)), ((), ())), preferred_element_type=jnp.float32)


def framed_outer(left, right, late, w0, w1):
    zero = jnp.zeros_like(left)
    first = mm(jnp.where(late, zero, left), right, 0, 0)
    second = mm(jnp.where(late, left, zero), right, 0, 0)
    return (w0 * first + w1 * second).astype(jnp.bfloat16)


def pre_kernel(heads, dim, scal, late_ref, key, value, previous, taps, conv, state, padded):
    count, channels = value.shape
    tap_count = taps.shape[0]
    padded[8 - (tap_count - 1) : 8, :] = previous[...].astype(jnp.float32)
    for c in chunks(channels, 256):
        padded[8:, c] = value[:, c].astype(jnp.float32)
        total = taps[0:1, c] * padded[8:, c]
        for j in range(1, tap_count):
            total = total + taps[j : j + 1, c] * padded[8 - j : 8 - j + count, c]
        conv[:, c] = total.astype(jnp.bfloat16)
    late = late_ref[...] > 0
    for h in range(heads):
        c = slice(h * dim, (h + 1) * dim)
        state[c, :] = framed_outer(key[:, c], conv[:, c], late, scal[0, h], 1.0)
    state[heads * dim :, :] = jnp.zeros_like(state[heads * dim :, :])


def mid_kernel(heads, dim, scal, late_ref, same, cross, query, key, conv, upstream, gain, state,
               grad_query, key_part, value_part, adjoint, terms):
    late = late_ref[...] > 0
    for h in range(heads):
        c = slice(h * dim, (h + 1) * dim)
        q, k, v, s_in = query[:, c], key[:, c], conv[:, c], state[c, :]
        row_scale = jnp.where(late, scal[2, h], scal[1, h])
        weight = same[...] + scal[0, h] * cross[...]
        attn = (mm(q, k, 1, 1) * weight).astype(jnp.bfloat16)
        numerator = mm(attn, v, 1, 0) + row_scale * mm(q, s_in, 1, 0)
        inv_rms = lax.rsqrt(jnp.mean(numerator * numerator, axis=1, keepdims=True) + EPSILON)
        normed = numerator * inv_rms
        up = upstream[:, c].astype(jnp.float32)
        terms[:, c] = jnp.sum(up * normed, axis=0, keepdims=True)
        normed_grad = up * gain[:, c]
        g = (inv_rms * (
            normed_grad - normed * jnp.mean(normed_grad * normed, axis=1, keepdims=True)
        )).astype(jnp.bfloat16)
        adjoint[c, :] = framed_outer(q, g, late, scal[1, h], scal[2, h])
        score = (mm(g, v, 1, 1) * weight).astype(jnp.bfloat16)
        grad_query[:, c] = (mm(score, k, 1, 0) + row_scale * mm(g, s_in, 1, 1)).astype(jnp.bfloat16)
        key_part[:, c] = mm(score, q, 0, 0)
        value_part[:, c] = mm(attn, g, 0, 0)
    adjoint[heads * dim :, :] = jnp.zeros_like(adjoint[heads * dim :, :])


def post_kernel(heads, dim, scal, late_ref, key, conv, value, previous, taps, adjoint, key_part, value_part,
                grad_key, grad_value, tap_terms, edge, last, padded, grads):
    count, channels = value.shape
    tap_count = taps.shape[0]
    late = late_ref[...] > 0
    for h in range(heads):
        c = slice(h * dim, (h + 1) * dim)
        into_end = jnp.where(late, 1.0, scal[0, h])
        adj = adjoint[c, :]
        grad_key[:, c] = (key_part[:, c] + into_end * mm(conv[:, c], adj, 1, 1)).astype(jnp.bfloat16)
        grads[:count, c] = value_part[:, c] + into_end * mm(key[:, c], adj, 1, 0)
    grads[count:, :] = jnp.zeros_like(grads[count:, :])
    edge[...] = grads[: tap_count - 1, :]
    padded[8 - (tap_count - 1) : 8, :] = previous[...].astype(jnp.float32)
    for c in chunks(channels, 256):
        padded[8:, c] = value[:, c].astype(jnp.float32)
        own = grads[:count, c]
        total = taps[0:1, c] * own
        tap_terms[0:1, c] = jnp.sum(own * padded[8:, c], axis=0, keepdims=True)
        for j in range(1, tap_count):
            total = total + taps[j : j + 1, c] * grads[j : j + count, c]
            tap_terms[j : j + 1, c] = jnp.sum(own * padded[8 - j : 8 - j + count, c], axis=0, keepdims=True)
        grad_value[:, c] = total.astype(jnp.bfloat16)
        last[:, c] = total[count - 8 :, :]


def local_call(kernel, name, args, outs, scratch=()):
    vmem = pl.BlockSpec(memory_space=pltpu.VMEM)
    return pl.pallas_call(
        kernel,
        out_shape=tuple(outs),
        in_specs=[pl.BlockSpec(memory_space=pltpu.SMEM)] + [vmem] * (len(args) - 1),
        out_specs=tuple([vmem] * len(outs)),
        scratch_shapes=list(scratch),
        compiler_params=pltpu.CompilerParams(vmem_limit_bytes=56 << 20),
        name=name,
    )(*args)


def body(
    queries,
    key_rows,
    value_rows,
    frame_len,
    log_decay,
    timestep,
    conv_kernel,
    norm_gain,
    mod_table,
    out_grad,
):
    f32, bf16 = jnp.float32, jnp.bfloat16
    shape = jax.ShapeDtypeStruct
    row_count, channels = queries.shape
    head_count = log_decay.shape[2]
    head_dim = channels // head_count
    score_scale = head_dim ** (-0.5)
    tap_count = conv_kernel.shape[0]
    block_count = lax.axis_size("seq")
    place = lax.axis_index("seq")
    state_rows = -(-channels // (16 * block_count)) * 16 * block_count

    previous = passed_along(value_rows[row_count - (tap_count - 1) :], "seq")
    cum0 = log_decay[0, 0]
    cum1 = cum0 + log_decay[0, 1]
    scal = jnp.stack([jnp.exp(cum1 - cum0), score_scale * jnp.exp(cum0), score_scale * jnp.exp(cum1)])
    first = frame_len[0, 0]
    late_at = lambda size, axis: (lax.broadcasted_iota(jnp.int32, size, axis) >= first).astype(jnp.int32)
    late = late_at((row_count, head_dim), 0)
    square = (row_count, row_count)
    late_t, late_s = late_at(square, 0), late_at(square, 1)
    same = jnp.where(late_t == late_s, score_scale, 0.0).astype(f32)
    cross = jnp.where(late_t > late_s, score_scale, 0.0).astype(f32)
    levels = jnp.arange(mod_table.shape[0], dtype=jnp.int32)
    mod_row = lax.dynamic_index_in_dim(mod_table, timestep[0], 0, True)
    gain = norm_gain[None, :] * (1.0 + mod_row)
    lanes = jnp.concatenate([
        cum1, timestep.astype(f32), jnp.zeros((128 - head_count - 1,), f32)])[None, :]

    conv_values, local_state = local_call(
        functools.partial(pre_kernel, head_count, head_dim), "conv_state",
        (scal, late, key_rows, value_rows, previous, conv_kernel),
        (shape((row_count, channels), bf16), shape((state_rows, head_dim), bf16)),
        [pltpu.VMEM((row_count + 8, channels), f32)])
    state_in, gathered = carried(local_state, lanes, None, head_dim, False)
    query_grad, key_part, value_part, adjoint_local, block_terms = local_call(
        functools.partial(mid_kernel, head_count, head_dim), "heads",
        (scal, late, same, cross, queries, key_rows, conv_values, out_grad, gain, state_in),
        (shape((row_count, channels), bf16), shape((row_count, channels), f32),
         shape((row_count, channels), f32), shape((state_rows, head_dim), bf16), shape((1, channels), f32)))
    adjoint, terms_all = carried(adjoint_local, block_terms, gathered, head_dim, True)
    key_grad, value_grad, tap_terms, edge, last = local_call(
        functools.partial(post_kernel, head_count, head_dim), "adjoint_terms",
        (scal, late, key_rows, conv_values, value_rows, previous, conv_kernel, adjoint, key_part, value_part),
        (shape((row_count, channels), bf16), shape((row_count, channels), bf16),
         shape((tap_count, channels), f32), shape((tap_count - 1, channels), f32), shape((8, channels), f32)),
        [pltpu.VMEM((row_count + 8, channels), f32)] * 2)
    kernel_sum, following = tail_exchange(tap_terms, edge)
    following = jnp.where(place == block_count - 1, 0.0, following)
    span = tap_count - 1
    ending = []
    for i in range(span):
        row = last[8 - span + i]
        for j in range(span - i, tap_count):
            row = row + conv_kernel[j] * following[i + j - span]
        ending.append(row)
    value_grad = lax.dynamic_update_slice(
        value_grad, jnp.stack(ending).astype(bf16), (row_count - span, 0))
    terms = terms_all[:, 0, :]
    chosen = (gathered[:, 0, head_count].astype(jnp.int32)[:, None] == levels[None, :]).astype(f32)
    sums = jnp.einsum("bl,bc->lc", chosen, terms, precision=lax.Precision.HIGHEST)
    gain_sum = jnp.sum(sums * (1.0 + mod_table), axis=0)
    table_sum = sums * norm_gain
    return (
        query_grad,
        key_grad,
        value_grad,
        kernel_sum / block_count,
        gain_sum / block_count,
        table_sum / block_count,
    )


def solution(mesh):
    in_specs = (
        P(("groups", "seq"), None),
        P(("groups", "seq"), None),
        P(("groups", "seq"), None),
        P(("groups", "seq"), None),
        P(("groups", "seq"), None, None),
        P(("groups", "seq")),
        P(),
        P(),
        P(),
        P(("groups", "seq"), None),
    )
    out_specs = (
        P(("groups", "seq"), None),
        P(("groups", "seq"), None),
        P(("groups", "seq"), None),
        P("groups", None),
        P("groups"),
        P("groups", None),
    )
    return jax.shard_map(body, mesh=mesh, in_specs=in_specs, out_specs=out_specs, check_vma=False)
```

```python
import functools

import jax
import jax.numpy as jnp
from jax import lax
from jax.experimental import pallas as pl
from jax.experimental.pallas import tpu as pltpu
from jax.sharding import PartitionSpec as P

EPSILON = 1e-06
MESH = pl.DeviceIdType.MESH


def scan_kernel(n, rows, head_dim, reverse, *refs):
    if reverse:
        (pieces, extra, decays, out, extra_all, inbox, outbox) = refs[:7]
    else:
        (pieces, extra, out, extra_all, inbox, outbox) = refs[:6]
        decays = extra_all
    (in_send, in_recv, ex_send, ex_recv, out_send, out_recv) = refs[-6:]
    me = lax.axis_index("seq")
    group = lax.axis_index("groups")

    def where(peer):
        return (group, peer)

    def piece_copy(peer, slot):
        return pltpu.make_async_remote_copy(
            src_ref=pieces.at[peer], dst_ref=inbox.at[slot],
            send_sem=in_send.at[peer], recv_sem=in_recv.at[slot],
            device_id=where(peer), device_id_type=MESH)

    def extra_copy(peer, slot):
        return pltpu.make_async_remote_copy(
            src_ref=extra, dst_ref=extra_all.at[slot],
            send_sem=ex_send.at[peer], recv_sem=ex_recv.at[slot],
            device_id=where(peer), device_id_type=MESH)

    def result_copy(peer, slot):
        return pltpu.make_async_remote_copy(
            src_ref=outbox.at[peer], dst_ref=out.at[slot],
            send_sem=out_send.at[peer], recv_sem=out_recv.at[slot],
            device_id=where(peer), device_id_type=MESH)

    barrier = pltpu.get_barrier_semaphore()

    def greet(k, c):
        pl.semaphore_signal(barrier, inc=1, device_id=where(lax.rem(me + k, n)), device_id_type=MESH)
        return c

    lax.fori_loop(1, n, greet, 0)
    inbox[me] = pieces[me]
    extra_all[me] = extra[...]
    pl.semaphore_wait(barrier, n - 1)

    def send(k, c):
        peer = lax.rem(me + k, n)
        extra_copy(peer, me).start()
        piece_copy(peer, me).start()
        return c

    lax.fori_loop(1, n, send, 0)

    lane = lax.broadcasted_iota(jnp.int32, (rows, 128), 1) * head_dim
    index = lax.broadcasted_iota(jnp.int32, (rows, 128), 0) + me * rows
    mine = (index >= lane) & (index < lane + head_dim)

    def step(i, state):
        b = n - 1 - i if reverse else i

        @pl.when(b != me)
        def _():
            extra_copy(b, b).wait_recv()
            piece_copy(b, b).wait_recv()

        outbox[b] = state.astype(jnp.bfloat16)

        @pl.when(b != me)
        def _():
            result_copy(b, me).start()

        row = decays[b]
        factor = jnp.exp(jnp.sum(jnp.where(mine, row, 0.0), axis=1, keepdims=True))
        return factor * state + inbox[b].astype(jnp.float32)

    lax.fori_loop(0, n, step, jnp.zeros(inbox.shape[1:], jnp.float32))
    out[me] = outbox[me]

    def finish(k, c):
        peer = lax.rem(me + k, n)
        extra_copy(peer, peer).wait_send()
        piece_copy(peer, peer).wait_send()
        result_copy(peer, peer).wait_send()
        result_copy(peer, peer).wait_recv()
        return c

    lax.fori_loop(1, n, finish, 0)


def carried(flat, extra, decays, depth, reverse):
    n = lax.axis_size("seq")
    rows, width = flat.shape[0] // n, flat.shape[1]
    pieces = flat.reshape(n, rows, width)
    vmem = pl.BlockSpec(memory_space=pltpu.VMEM)
    args = (pieces, extra) + ((decays,) if reverse else ())
    out, gathered = pl.pallas_call(
        functools.partial(scan_kernel, n, rows, depth, reverse),
        out_shape=(
            jax.ShapeDtypeStruct((n, rows, width), jnp.bfloat16),
            jax.ShapeDtypeStruct((n,) + extra.shape, jnp.float32),
        ),
        in_specs=[vmem] * len(args),
        out_specs=(vmem, vmem),
        scratch_shapes=[pltpu.VMEM((n, rows, width), jnp.bfloat16)] * 2
        + [pltpu.SemaphoreType.DMA((n,))] * 6,
        compiler_params=pltpu.CompilerParams(
            collective_id=1 if reverse else 0, has_side_effects=True, vmem_limit_bytes=48 << 20),
        name="adjoint_scan" if reverse else "state_scan",
    )(*args)
    return out.reshape(n * rows, width), gathered


def tail_kernel(n, terms, edge, total, following, held, landed, send_sem, recv_sem, edge_send, edge_recv):
    me = lax.axis_index("seq")
    group = lax.axis_index("groups")
    steps = n.bit_length() - 1
    barrier = pltpu.get_barrier_semaphore()
    partners = [me + (1 << i) - (2 << i) * ((me // (1 << i)) % 2) for i in range(steps)]
    for partner in partners:
        pl.semaphore_signal(barrier, inc=1, device_id=(group, partner), device_id_type=MESH)
    before, after = lax.rem(me + n - 1, n), lax.rem(me + 1, n)
    for peer in (before, after):
        pl.semaphore_signal(barrier, inc=1, device_id=(group, peer), device_id_type=MESH)
    pl.semaphore_wait(barrier, steps + 2)
    edge_copy = pltpu.make_async_remote_copy(
        src_ref=edge, dst_ref=following, send_sem=edge_send, recv_sem=edge_recv,
        device_id=(group, before), device_id_type=MESH)
    edge_copy.start()
    held[0] = terms[...]
    for i, partner in enumerate(partners):
        copy = pltpu.make_async_remote_copy(
            src_ref=held.at[i], dst_ref=landed.at[i], send_sem=send_sem.at[i], recv_sem=recv_sem.at[i],
            device_id=(group, partner), device_id_type=MESH)
        copy.start()
        copy.wait()
        held[i + 1] = held[i] + landed[i]
    total[...] = held[steps]
    edge_copy.wait()


def tail_exchange(terms, edge):
    n = lax.axis_size("seq")
    steps = n.bit_length() - 1
    vmem = pl.BlockSpec(memory_space=pltpu.VMEM)
    return pl.pallas_call(
        functools.partial(tail_kernel, n),
        out_shape=(jax.ShapeDtypeStruct(terms.shape, jnp.float32), jax.ShapeDtypeStruct(edge.shape, jnp.float32)),
        in_specs=[vmem, vmem],
        out_specs=(vmem, vmem),
        scratch_shapes=[
            pltpu.VMEM((steps + 1,) + terms.shape, jnp.float32),
            pltpu.VMEM((steps,) + terms.shape, jnp.float32),
            pltpu.SemaphoreType.DMA((steps,)),
            pltpu.SemaphoreType.DMA((steps,)),
            pltpu.SemaphoreType.DMA,
            pltpu.SemaphoreType.DMA,
        ],
        compiler_params=pltpu.CompilerParams(collective_id=2, has_side_effects=True),
        name="tail_exchange",
    )(terms, edge)


def passed_along(value, axis):
    count = lax.axis_size(axis)
    return lax.ppermute(value, axis, [(s, s + 1) for s in range(count - 1)])


def mm(a, b, ca, cb):
    return lax.dot_general(a, b, (((ca,), (cb,)), ((), ())), preferred_element_type=jnp.float32)


def framed_outer(left, right, late, w0, w1):
    second = right * late
    first = right - second
    return (w0 * mm(left, first, 1, 1) + w1 * mm(left, second, 1, 1)).astype(jnp.bfloat16)


def per_head(heads, dim, work):
    def pair(i, carry):
        for j in range(2):
            h = i * 2 + j
            work(h, pl.ds(pl.multiple_of(h * dim, 16), dim))
        return carry

    lax.fori_loop(0, heads // 2, pair, 0)
    if heads % 2:
        work(heads - 1, pl.ds((heads - 1) * dim, dim))


def delayed(value, before, taps):
    count = value.shape[1]
    joined = jnp.concatenate([before, value], axis=1)
    width = joined.shape[1]
    return [value] + [pltpu.roll(joined, j, 1)[:, width - count :] for j in range(1, taps)]


def pre_kernel(heads, dim, tap_count, scal, late, key, value, before, columns, conv, state):
    def work(h, c):
        x = delayed(value[c, :].astype(jnp.float32), before[c, :].astype(jnp.float32), tap_count)
        cols = columns[c, :]
        total = cols[:, 0:1] * x[0]
        for j in range(1, tap_count):
            total = total + cols[:, j : j + 1] * x[j]
        v = total.astype(jnp.bfloat16)
        conv[c, :] = v
        state[c, :] = framed_outer(v, key[c, :], late[...], scal[0, h], 1.0)

    per_head(heads, dim, work)
    state[heads * dim :, :] = jnp.zeros_like(state[heads * dim :, :])


def mid_kernel(heads, dim, tap_count, scal, late, same, cross, query, key, conv, upstream, columns, state,
               grad_query, key_part, value_part, adjoint, terms):
    is_late = late[0:1, :].astype(jnp.float32) > 0.5

    def work(h, c):
        q, k, v, s_in = query[c, :], key[c, :], conv[c, :], state[c, :]
        row_scale = jnp.where(is_late, scal[2, h], scal[1, h])
        weight = same[...] + scal[0, h] * cross[...]
        attn = (mm(k, q, 0, 0) * weight).astype(jnp.bfloat16)
        numerator = mm(v, attn, 1, 0) + row_scale * mm(s_in, q, 1, 0)
        inv_rms = lax.rsqrt(jnp.mean(numerator * numerator, axis=0, keepdims=True) + EPSILON)
        normed = numerator * inv_rms
        up = upstream[c, :].astype(jnp.float32)
        terms[c, :] = jnp.sum(up * normed, axis=1, keepdims=True)
        normed_grad = up * columns[c, :][:, tap_count : tap_count + 1]
        g = (inv_rms * (
            normed_grad - normed * jnp.mean(normed_grad * normed, axis=0, keepdims=True)
        )).astype(jnp.bfloat16)
        adjoint[c, :] = framed_outer(g, q, late[...], scal[1, h], scal[2, h])
        score = (mm(v, g, 0, 0) * weight).astype(jnp.bfloat16)
        grad_query[c, :] = (mm(k, score, 1, 0) + row_scale * mm(s_in, g, 0, 0)).astype(jnp.bfloat16)
        key_part[c, :] = mm(q, score, 1, 1)
        value_part[c, :] = mm(g, attn, 1, 1)

    per_head(heads, dim, work)
    adjoint[heads * dim :, :] = jnp.zeros_like(adjoint[heads * dim :, :])


def post_kernel(heads, dim, tap_count, scal, late, key, conv, value, before, columns, adjoint, key_part,
                value_part, grad_key, grad_value, tap_terms, opening, ending):
    is_late = late[0:1, :].astype(jnp.float32) > 0.5

    def work(h, c):
        into_end = jnp.where(is_late, 1.0, scal[0, h])
        adj = adjoint[c, :]
        grad_key[c, :] = (key_part[c, :] + into_end * mm(adj, conv[c, :], 0, 0)).astype(jnp.bfloat16)
        own = value_part[c, :] + into_end * mm(adj, key[c, :], 1, 0)
        opening[c, :] = own[:, :128]
        count = own.shape[1]
        x = delayed(value[c, :].astype(jnp.float32), before[c, :].astype(jnp.float32), tap_count)
        joined = jnp.concatenate([own, jnp.zeros((dim, 128), jnp.float32)], axis=1)
        cols = columns[c, :]
        total = cols[:, 0:1] * own
        tap_terms[c, 0:1] = jnp.sum(own * x[0], axis=1, keepdims=True)
        for j in range(1, tap_count):
            total = total + cols[:, j : j + 1] * pltpu.roll(joined, count + 128 - j, 1)[:, :count]
            tap_terms[c, j : j + 1] = jnp.sum(own * x[j], axis=1, keepdims=True)
        grad_value[c, :] = total.astype(jnp.bfloat16)
        ending[c, :] = total[:, count - 128 :]

    per_head(heads, dim, work)


def local_call(kernel, name, args, outs, scratch=()):
    vmem = pl.BlockSpec(memory_space=pltpu.VMEM)
    return pl.pallas_call(
        kernel,
        out_shape=tuple(outs),
        in_specs=[pl.BlockSpec(memory_space=pltpu.SMEM)] + [vmem] * (len(args) - 1),
        out_specs=tuple([vmem] * len(outs)),
        scratch_shapes=list(scratch),
        compiler_params=pltpu.CompilerParams(vmem_limit_bytes=56 << 20),
        name=name,
    )(*args)


def body(
    queries,
    key_rows,
    value_rows,
    frame_len,
    log_decay,
    timestep,
    conv_kernel,
    norm_gain,
    mod_table,
    out_grad,
):
    f32, bf16 = jnp.float32, jnp.bfloat16
    shape = jax.ShapeDtypeStruct
    row_count, channels = queries.shape
    head_count = log_decay.shape[2]
    head_dim = channels // head_count
    score_scale = head_dim ** (-0.5)
    tap_count = conv_kernel.shape[0]
    block_count = lax.axis_size("seq")
    place = lax.axis_index("seq")
    state_rows = -(-channels // (16 * block_count)) * 16 * block_count

    span = tap_count - 1
    previous = passed_along(value_rows[row_count - span :], "seq")
    before = jnp.pad(previous.T, ((0, 0), (128 - span, 0)))
    query_t, key_t, value_t, upstream_t = (a.T for a in (queries, key_rows, value_rows, out_grad))
    cum0 = log_decay[0, 0]
    cum1 = cum0 + log_decay[0, 1]
    scal = jnp.stack([jnp.exp(cum1 - cum0), score_scale * jnp.exp(cum0), score_scale * jnp.exp(cum1)])
    first = frame_len[0, 0]
    late_at = lambda size, axis: lax.broadcasted_iota(jnp.int32, size, axis) >= first
    late = late_at((head_dim, row_count), 1).astype(bf16)
    square = (row_count, row_count)
    late_s, late_t = late_at(square, 0), late_at(square, 1)
    same = jnp.where(late_t == late_s, score_scale, 0.0).astype(f32)
    cross = jnp.where(late_t & ~late_s, score_scale, 0.0).astype(f32)
    levels = jnp.arange(mod_table.shape[0], dtype=jnp.int32)
    mod_row = lax.dynamic_index_in_dim(mod_table, timestep[0], 0, True)
    gain = norm_gain[None, :] * (1.0 + mod_row)
    columns = jnp.concatenate([conv_kernel, gain], axis=0).T
    lanes = jnp.concatenate([
        cum1, timestep.astype(f32), jnp.zeros((128 - head_count - 1,), f32)])[None, :]

    sizes = (head_count, head_dim, tap_count)
    whole = (channels, row_count)
    conv_values, local_state = local_call(
        functools.partial(pre_kernel, *sizes), "conv_state",
        (scal, late, key_t, value_t, before, columns),
        (shape(whole, bf16), shape((state_rows, head_dim), bf16)))
    state_in, gathered = carried(local_state, lanes, None, head_dim, False)
    query_grad, key_part, value_part, adjoint_local, block_terms = local_call(
        functools.partial(mid_kernel, *sizes), "heads",
        (scal, late, same, cross, query_t, key_t, conv_values, upstream_t, columns, state_in),
        (shape(whole, bf16), shape(whole, f32), shape(whole, f32),
         shape((state_rows, head_dim), bf16), shape((channels, 1), f32)))
    adjoint, terms_all = carried(adjoint_local, block_terms.reshape(1, channels), gathered, head_dim, True)
    key_grad, value_grad, tap_terms, opening, ending = local_call(
        functools.partial(post_kernel, *sizes), "adjoint_terms",
        (scal, late, key_t, conv_values, value_t, before, columns, adjoint, key_part, value_part),
        (shape(whole, bf16), shape(whole, bf16), shape((channels, tap_count), f32),
         shape((channels, 128), f32), shape((channels, 128), f32)))
    kernel_sum, following = tail_exchange(tap_terms.T, opening[:, :span].T)
    following = jnp.where(place == block_count - 1, 0.0, following).T
    fixed = []
    for i in range(span):
        column = ending[:, 128 - span + i]
        for j in range(span - i, tap_count):
            column = column + conv_kernel[j] * following[:, i + j - span]
        fixed.append(column)
    value_grad = lax.dynamic_update_slice(
        value_grad, jnp.stack(fixed, axis=1).astype(bf16), (0, row_count - span))
    query_grad, key_grad, value_grad = query_grad.T, key_grad.T, value_grad.T
    terms = terms_all[:, 0, :]
    chosen = (gathered[:, 0, head_count].astype(jnp.int32)[:, None] == levels[None, :]).astype(f32)
    sums = jnp.einsum("bl,bc->lc", chosen, terms, precision=lax.Precision.HIGHEST)
    gain_sum = jnp.sum(sums * (1.0 + mod_table), axis=0)
    table_sum = sums * norm_gain
    return (
        query_grad,
        key_grad,
        value_grad,
        kernel_sum / block_count,
        gain_sum / block_count,
        table_sum / block_count,
    )


def solution(mesh):
    in_specs = (
        P(("groups", "seq"), None),
        P(("groups", "seq"), None),
        P(("groups", "seq"), None),
        P(("groups", "seq"), None),
        P(("groups", "seq"), None, None),
        P(("groups", "seq")),
        P(),
        P(),
        P(),
        P(("groups", "seq"), None),
    )
    out_specs = (
        P(("groups", "seq"), None),
        P(("groups", "seq"), None),
        P(("groups", "seq"), None),
        P("groups", None),
        P("groups"),
        P("groups", None),
    )
    return jax.shard_map(body, mesh=mesh, in_specs=in_specs, out_specs=out_specs, check_vma=False)
```

```python
import functools

import jax
import jax.numpy as jnp
from jax import lax
from jax.experimental import pallas as pl
from jax.experimental.pallas import tpu as pltpu
from jax.sharding import PartitionSpec as P

EPSILON = 1e-06
MESH = pl.DeviceIdType.MESH


def scan_kernel(n, rows, heads, head_dim, reverse, work, ins, outs, *refs):
    lead = 3 if reverse else 2
    work = functools.partial(work, *refs[lead : lead + ins], *refs[lead + ins + 2 : lead + ins + 2 + outs])
    refs = refs[:lead] + refs[lead + ins : lead + ins + 2] + refs[lead + ins + 2 + outs :]
    if reverse:
        (pieces, extra, decays, out, extra_all, inbox, outbox) = refs[:7]
    else:
        (pieces, extra, out, extra_all, inbox, outbox) = refs[:6]
        decays = extra_all
    (in_send, in_recv, ex_send, ex_recv, out_send, out_recv) = refs[-6:]
    me = lax.axis_index("seq")
    group = lax.axis_index("groups")

    def where(peer):
        return (group, peer)

    def piece_copy(peer, slot):
        return pltpu.make_async_remote_copy(
            src_ref=pieces.at[peer], dst_ref=inbox.at[slot],
            send_sem=in_send.at[peer], recv_sem=in_recv.at[slot],
            device_id=where(peer), device_id_type=MESH)

    def extra_copy(peer, slot):
        return pltpu.make_async_remote_copy(
            src_ref=extra, dst_ref=extra_all.at[slot],
            send_sem=ex_send.at[peer], recv_sem=ex_recv.at[slot],
            device_id=where(peer), device_id_type=MESH)

    def result_copy(peer, slot):
        return pltpu.make_async_remote_copy(
            src_ref=outbox.at[peer], dst_ref=out.at[slot],
            send_sem=out_send.at[peer], recv_sem=out_recv.at[slot],
            device_id=where(peer), device_id_type=MESH)

    barrier = pltpu.get_barrier_semaphore()

    def greet(k, c):
        pl.semaphore_signal(barrier, inc=1, device_id=where(lax.rem(me + k, n)), device_id_type=MESH)
        return c

    lax.fori_loop(1, n, greet, 0)
    inbox[me] = pieces[me]
    extra_all[me] = extra[...]
    pl.semaphore_wait(barrier, n - 1)

    def send(k, c):
        peer = lax.rem(me + k, n)
        extra_copy(peer, me).start()
        piece_copy(peer, me).start()
        return c

    lax.fori_loop(1, n, send, 0)

    half = heads // 4 * 2
    per_head(0, half, head_dim, work)
    lane = lax.broadcasted_iota(jnp.int32, (rows, 128), 1) * head_dim
    index = lax.broadcasted_iota(jnp.int32, (rows, 128), 0) + me * rows
    mine = (index >= lane) & (index < lane + head_dim)

    def step(i, state):
        b = n - 1 - i if reverse else i

        @pl.when(b != me)
        def _():
            extra_copy(b, b).wait_recv()
            piece_copy(b, b).wait_recv()

        outbox[b] = state.astype(jnp.bfloat16)

        @pl.when(b != me)
        def _():
            result_copy(b, me).start()

        row = decays[b]
        factor = jnp.exp(jnp.sum(jnp.where(mine, row, 0.0), axis=1, keepdims=True))
        return factor * state + inbox[b].astype(jnp.float32)

    lax.fori_loop(0, n, step, jnp.zeros(inbox.shape[1:], jnp.float32))
    out[me] = outbox[me]
    per_head(half, heads, head_dim, work)

    def finish(k, c):
        peer = lax.rem(me + k, n)
        extra_copy(peer, peer).wait_send()
        piece_copy(peer, peer).wait_send()
        result_copy(peer, peer).wait_send()
        result_copy(peer, peer).wait_recv()
        return c

    lax.fori_loop(1, n, finish, 0)


def carried(flat, extra, decays, heads, depth, reverse, work, work_args, work_outs):
    n = lax.axis_size("seq")
    rows, width = flat.shape[0] // n, flat.shape[1]
    pieces = flat.reshape(n, rows, width)
    vmem = pl.BlockSpec(memory_space=pltpu.VMEM)
    args = (pieces, extra) + ((decays,) if reverse else ()) + tuple(work_args)
    out, gathered, *results = pl.pallas_call(
        functools.partial(scan_kernel, n, rows, heads, depth, reverse, work, len(work_args), len(work_outs)),
        out_shape=(
            jax.ShapeDtypeStruct((n, rows, width), jnp.bfloat16),
            jax.ShapeDtypeStruct((n,) + extra.shape, jnp.float32),
        ) + tuple(work_outs),
        in_specs=[vmem] * (len(args) - len(work_args)) + [pl.BlockSpec(memory_space=pltpu.SMEM)]
        + [vmem] * (len(work_args) - 1),
        out_specs=(vmem,) * (2 + len(work_outs)),
        scratch_shapes=[pltpu.VMEM((n, rows, width), jnp.bfloat16)] * 2
        + [pltpu.SemaphoreType.DMA((n,))] * 6,
        compiler_params=pltpu.CompilerParams(
            collective_id=1 if reverse else 0, has_side_effects=True, vmem_limit_bytes=48 << 20),
        name="adjoint_scan" if reverse else "state_scan",
    )(*args)
    return (out.reshape(n * rows, width), gathered, *results)


def tail_kernel(n, terms, edge, total, following, held, landed, send_sem, recv_sem, edge_send, edge_recv):
    me = lax.axis_index("seq")
    group = lax.axis_index("groups")
    steps = n.bit_length() - 1
    barrier = pltpu.get_barrier_semaphore()
    partners = [me + (1 << i) - (2 << i) * ((me // (1 << i)) % 2) for i in range(steps)]
    for partner in partners:
        pl.semaphore_signal(barrier, inc=1, device_id=(group, partner), device_id_type=MESH)
    before, after = lax.rem(me + n - 1, n), lax.rem(me + 1, n)
    for peer in (before, after):
        pl.semaphore_signal(barrier, inc=1, device_id=(group, peer), device_id_type=MESH)
    pl.semaphore_wait(barrier, steps + 2)
    edge_copy = pltpu.make_async_remote_copy(
        src_ref=edge, dst_ref=following, send_sem=edge_send, recv_sem=edge_recv,
        device_id=(group, before), device_id_type=MESH)
    edge_copy.start()
    held[0] = terms[...]
    for i, partner in enumerate(partners):
        copy = pltpu.make_async_remote_copy(
            src_ref=held.at[i], dst_ref=landed.at[i], send_sem=send_sem.at[i], recv_sem=recv_sem.at[i],
            device_id=(group, partner), device_id_type=MESH)
        copy.start()
        copy.wait()
        held[i + 1] = held[i] + landed[i]
    total[...] = held[steps]
    edge_copy.wait()


def tail_exchange(terms, edge):
    n = lax.axis_size("seq")
    steps = n.bit_length() - 1
    vmem = pl.BlockSpec(memory_space=pltpu.VMEM)
    return pl.pallas_call(
        functools.partial(tail_kernel, n),
        out_shape=(jax.ShapeDtypeStruct(terms.shape, jnp.float32), jax.ShapeDtypeStruct(edge.shape, jnp.float32)),
        in_specs=[vmem, vmem],
        out_specs=(vmem, vmem),
        scratch_shapes=[
            pltpu.VMEM((steps + 1,) + terms.shape, jnp.float32),
            pltpu.VMEM((steps,) + terms.shape, jnp.float32),
            pltpu.SemaphoreType.DMA((steps,)),
            pltpu.SemaphoreType.DMA((steps,)),
            pltpu.SemaphoreType.DMA,
            pltpu.SemaphoreType.DMA,
        ],
        compiler_params=pltpu.CompilerParams(collective_id=2, has_side_effects=True),
        name="tail_exchange",
    )(terms, edge)


def passed_along(value, axis):
    count = lax.axis_size(axis)
    return lax.ppermute(value, axis, [(s, s + 1) for s in range(count - 1)])


def mm(a, b, ca, cb):
    return lax.dot_general(a, b, (((ca,), (cb,)), ((), ())), preferred_element_type=jnp.float32)


def framed_outer(left, right, late, w0, w1):
    second = right * late
    first = right - second
    return (w0 * mm(left, first, 1, 1) + w1 * mm(left, second, 1, 1)).astype(jnp.bfloat16)


def per_head(start, stop, dim, work):
    def pair(i, carry):
        for j in range(2):
            h = i * 2 + j
            work(h, pl.ds(pl.multiple_of(h * dim, 16), dim))
        return carry

    lax.fori_loop(start // 2, stop // 2, pair, 0)
    if stop % 2:
        work(stop - 1, pl.ds((stop - 1) * dim, dim))


def delayed(value, before, taps):
    count = value.shape[1]
    joined = jnp.concatenate([before, value], axis=1)
    width = joined.shape[1]
    return [value] + [pltpu.roll(joined, j, 1)[:, width - count :] for j in range(1, taps)]


def pre_kernel(heads, dim, tap_count, scal, late, key, value, before, columns, conv, state):
    def work(h, c):
        x = delayed(value[c, :].astype(jnp.float32), before[c, :].astype(jnp.float32), tap_count)
        cols = columns[c, :]
        total = cols[:, 0:1] * x[0]
        for j in range(1, tap_count):
            total = total + cols[:, j : j + 1] * x[j]
        v = total.astype(jnp.bfloat16)
        conv[c, :] = v
        state[c, :] = framed_outer(v, key[c, :], late[...], scal[0, h], 1.0)

    per_head(0, heads, dim, work)
    state[heads * dim :, :] = jnp.zeros_like(state[heads * dim :, :])


def ahead_work(scal, same, cross, query, key, conv, part, h, c):
    weight = same[...] + scal[0, h] * cross[...]
    attn = (mm(key[c, :], query[c, :], 0, 0) * weight).astype(jnp.bfloat16)
    part[c, :] = mm(conv[c, :], attn, 1, 0)


def back_work(scal, late, same, cross, query, key, conv, grad, state, grad_query, key_part, value_part, h, c):
    row_scale = jnp.where(late[0:1, :].astype(jnp.float32) > 0.5, scal[2, h], scal[1, h])
    q, k, g = query[c, :], key[c, :], grad[c, :]
    weight = same[...] + scal[0, h] * cross[...]
    attn = (mm(k, q, 0, 0) * weight).astype(jnp.bfloat16)
    score = (mm(conv[c, :], g, 0, 0) * weight).astype(jnp.bfloat16)
    grad_query[c, :] = (mm(k, score, 1, 0) + row_scale * mm(state[c, :], g, 0, 0)).astype(jnp.bfloat16)
    key_part[c, :] = mm(q, score, 1, 1)
    value_part[c, :] = mm(g, attn, 1, 1)


def mid_kernel(heads, dim, tap_count, scal, late, query, part, upstream, columns, state, grad, adjoint, terms):
    is_late = late[0:1, :].astype(jnp.float32) > 0.5

    def work(h, c):
        q = query[c, :]
        row_scale = jnp.where(is_late, scal[2, h], scal[1, h])
        numerator = part[c, :] + row_scale * mm(state[c, :], q, 1, 0)
        inv_rms = lax.rsqrt(jnp.mean(numerator * numerator, axis=0, keepdims=True) + EPSILON)
        normed = numerator * inv_rms
        up = upstream[c, :].astype(jnp.float32)
        terms[c, :] = jnp.sum(up * normed, axis=1, keepdims=True)
        normed_grad = up * columns[c, :][:, tap_count : tap_count + 1]
        g = (inv_rms * (
            normed_grad - normed * jnp.mean(normed_grad * normed, axis=0, keepdims=True)
        )).astype(jnp.bfloat16)
        grad[c, :] = g
        adjoint[c, :] = framed_outer(g, q, late[...], scal[1, h], scal[2, h])

    per_head(0, heads, dim, work)
    adjoint[heads * dim :, :] = jnp.zeros_like(adjoint[heads * dim :, :])


def post_kernel(heads, dim, tap_count, scal, late, key, conv, value, before, columns, adjoint, key_part,
                value_part, grad_key, grad_value, tap_terms, opening, ending):
    is_late = late[0:1, :].astype(jnp.float32) > 0.5

    def work(h, c):
        into_end = jnp.where(is_late, 1.0, scal[0, h])
        adj = adjoint[c, :]
        grad_key[c, :] = (key_part[c, :] + into_end * mm(adj, conv[c, :], 0, 0)).astype(jnp.bfloat16)
        own = value_part[c, :] + into_end * mm(adj, key[c, :], 1, 0)
        opening[c, :] = own[:, :128]
        count = own.shape[1]
        x = delayed(value[c, :].astype(jnp.float32), before[c, :].astype(jnp.float32), tap_count)
        joined = jnp.concatenate([own, jnp.zeros((dim, 128), jnp.float32)], axis=1)
        cols = columns[c, :]
        total = cols[:, 0:1] * own
        tap_terms[c, 0:1] = jnp.sum(own * x[0], axis=1, keepdims=True)
        for j in range(1, tap_count):
            total = total + cols[:, j : j + 1] * pltpu.roll(joined, count + 128 - j, 1)[:, :count]
            tap_terms[c, j : j + 1] = jnp.sum(own * x[j], axis=1, keepdims=True)
        grad_value[c, :] = total.astype(jnp.bfloat16)
        ending[c, :] = total[:, count - 128 :]

    per_head(0, heads, dim, work)


def end_kernel(whole, tile, out):
    out[...] = tile[...].astype(jnp.bfloat16)


def local_call(kernel, name, args, outs, scratch=()):
    vmem = pl.BlockSpec(memory_space=pltpu.VMEM)
    return pl.pallas_call(
        kernel,
        out_shape=tuple(outs),
        in_specs=[pl.BlockSpec(memory_space=pltpu.SMEM)] + [vmem] * (len(args) - 1),
        out_specs=tuple([vmem] * len(outs)),
        scratch_shapes=list(scratch),
        compiler_params=pltpu.CompilerParams(vmem_limit_bytes=56 << 20),
        name=name,
    )(*args)


def body(
    queries,
    key_rows,
    value_rows,
    frame_len,
    log_decay,
    timestep,
    conv_kernel,
    norm_gain,
    mod_table,
    out_grad,
):
    f32, bf16 = jnp.float32, jnp.bfloat16
    shape = jax.ShapeDtypeStruct
    row_count, channels = queries.shape
    head_count = log_decay.shape[2]
    head_dim = channels // head_count
    score_scale = head_dim ** (-0.5)
    tap_count = conv_kernel.shape[0]
    block_count = lax.axis_size("seq")
    place = lax.axis_index("seq")
    state_rows = -(-channels // (16 * block_count)) * 16 * block_count

    span = tap_count - 1
    previous = passed_along(value_rows[row_count - span :], "seq")
    before = jnp.pad(previous.T, ((0, 0), (128 - span, 0)))
    query_t, key_t, value_t, upstream_t = (a.T for a in (queries, key_rows, value_rows, out_grad))
    cum0 = log_decay[0, 0]
    cum1 = cum0 + log_decay[0, 1]
    scal = jnp.stack([jnp.exp(cum1 - cum0), score_scale * jnp.exp(cum0), score_scale * jnp.exp(cum1)])
    first = frame_len[0, 0]
    late_at = lambda size, axis: lax.broadcasted_iota(jnp.int32, size, axis) >= first
    late = late_at((head_dim, row_count), 1).astype(bf16)
    square = (row_count, row_count)
    late_s, late_t = late_at(square, 0), late_at(square, 1)
    same = jnp.where(late_t == late_s, score_scale, 0.0).astype(f32)
    cross = jnp.where(late_t & ~late_s, score_scale, 0.0).astype(f32)
    levels = jnp.arange(mod_table.shape[0], dtype=jnp.int32)
    mod_row = lax.dynamic_index_in_dim(mod_table, timestep[0], 0, True)
    gain = norm_gain[None, :] * (1.0 + mod_row)
    columns = jnp.concatenate([conv_kernel, gain], axis=0).T
    lanes = jnp.concatenate([
        cum1, timestep.astype(f32), jnp.zeros((128 - head_count - 1,), f32)])[None, :]

    sizes = (head_count, head_dim, tap_count)
    whole = (channels, row_count)
    conv_values, local_state = local_call(
        functools.partial(pre_kernel, *sizes), "conv_state",
        (scal, late, key_t, value_t, before, columns),
        (shape(whole, bf16), shape((state_rows, head_dim), bf16)))
    state_in, gathered, part = carried(
        local_state, lanes, None, head_count, head_dim, False, ahead_work,
        (scal, same, cross, query_t, key_t, conv_values), (shape(whole, f32),))
    grad, adjoint_local, block_terms = local_call(
        functools.partial(mid_kernel, *sizes), "heads",
        (scal, late, query_t, part, upstream_t, columns, state_in),
        (shape(whole, bf16), shape((state_rows, head_dim), bf16), shape((channels, 1), f32)))
    adjoint, terms_all, query_grad, key_part, value_part = carried(
        adjoint_local, block_terms.reshape(1, channels), gathered, head_count, head_dim, True, back_work,
        (scal, late, same, cross, query_t, key_t, conv_values, grad, state_in),
        (shape(whole, bf16), shape(whole, f32), shape(whole, f32)))
    key_grad, value_grad, tap_terms, opening, ending = local_call(
        functools.partial(post_kernel, *sizes), "adjoint_terms",
        (scal, late, key_t, conv_values, value_t, before, columns, adjoint, key_part, value_part),
        (shape(whole, bf16), shape(whole, bf16), shape((channels, tap_count), f32),
         shape((channels, 128), f32), shape((channels, 128), f32)))
    kernel_sum, following = tail_exchange(tap_terms.T, opening[:, :span].T)
    following = jnp.where(place == block_count - 1, 0.0, following).T
    fixed = []
    for i in range(span):
        column = jnp.zeros((channels,), f32)
        for j in range(span - i, tap_count):
            column = column + conv_kernel[j] * following[:, i + j - span]
        fixed.append(column)
    tile = ending + jnp.pad(jnp.stack(fixed, axis=1), ((0, 0), (128 - span, 0)))
    value_grad = pl.pallas_call(
        end_kernel,
        grid=(1,),
        out_shape=shape(whole, bf16),
        in_specs=[pl.BlockSpec(memory_space=pl.ANY), pl.BlockSpec((channels, 128), lambda i: (0, 0))],
        out_specs=pl.BlockSpec((channels, 128), lambda i: (0, row_count // 128 - 1)),
        input_output_aliases={0: 0},
        name="last_tokens",
    )(value_grad, tile)
    query_grad, key_grad, value_grad = query_grad.T, key_grad.T, value_grad.T
    terms = terms_all[:, 0, :]
    chosen = (gathered[:, 0, head_count].astype(jnp.int32)[:, None] == levels[None, :]).astype(f32)
    sums = jnp.einsum("bl,bc->lc", chosen, terms, precision=lax.Precision.HIGHEST)
    gain_sum = jnp.sum(sums * (1.0 + mod_table), axis=0)
    table_sum = sums * norm_gain
    return (
        query_grad,
        key_grad,
        value_grad,
        kernel_sum / block_count,
        gain_sum / block_count,
        table_sum / block_count,
    )


def solution(mesh):
    in_specs = (
        P(("groups", "seq"), None),
        P(("groups", "seq"), None),
        P(("groups", "seq"), None),
        P(("groups", "seq"), None),
        P(("groups", "seq"), None, None),
        P(("groups", "seq")),
        P(),
        P(),
        P(),
        P(("groups", "seq"), None),
    )
    out_specs = (
        P(("groups", "seq"), None),
        P(("groups", "seq"), None),
        P(("groups", "seq"), None),
        P("groups", None),
        P("groups"),
        P("groups", None),
    )
    return jax.shard_map(body, mesh=mesh, in_specs=in_specs, out_specs=out_specs, check_vma=False)
```

```python
import functools

import jax
import jax.numpy as jnp
from jax import lax
from jax.experimental import pallas as pl
from jax.experimental.pallas import tpu as pltpu
from jax.sharding import PartitionSpec as P

EPSILON = 1e-06
MESH = pl.DeviceIdType.MESH


def scan_kernel(n, rows, heads, head_dim, reverse, work, ins, outs, *refs):
    lead = 3 if reverse else 2
    work = functools.partial(work, *refs[lead : lead + ins], *refs[lead + ins + 2 : lead + ins + 2 + outs])
    refs = refs[:lead] + refs[lead + ins : lead + ins + 2] + refs[lead + ins + 2 + outs :]
    if reverse:
        (pieces, extra, decays, out, extra_all, inbox, outbox) = refs[:7]
    else:
        (pieces, extra, out, extra_all, inbox, outbox) = refs[:6]
        decays = extra_all
    (in_send, in_recv, ex_send, ex_recv, out_send, out_recv) = refs[-6:]
    me = lax.axis_index("seq")
    group = lax.axis_index("groups")

    def where(peer):
        return (group, peer)

    def piece_copy(peer, slot):
        return pltpu.make_async_remote_copy(
            src_ref=pieces.at[peer], dst_ref=inbox.at[slot],
            send_sem=in_send.at[peer], recv_sem=in_recv.at[slot],
            device_id=where(peer), device_id_type=MESH)

    def extra_copy(peer, slot):
        return pltpu.make_async_remote_copy(
            src_ref=extra, dst_ref=extra_all.at[slot],
            send_sem=ex_send.at[peer], recv_sem=ex_recv.at[slot],
            device_id=where(peer), device_id_type=MESH)

    def result_copy(peer, slot):
        return pltpu.make_async_remote_copy(
            src_ref=outbox.at[peer], dst_ref=out.at[slot],
            send_sem=out_send.at[peer], recv_sem=out_recv.at[slot],
            device_id=where(peer), device_id_type=MESH)

    barrier = pltpu.get_barrier_semaphore()

    def greet(k, c):
        pl.semaphore_signal(barrier, inc=1, device_id=where(lax.rem(me + k, n)), device_id_type=MESH)
        return c

    lax.fori_loop(1, n, greet, 0)
    inbox[me] = pieces[me]
    extra_all[me] = extra[...]
    pl.semaphore_wait(barrier, n - 1)

    def send(k, c):
        peer = lax.rem(me + k, n)
        extra_copy(peer, me).start()
        piece_copy(peer, me).start()
        return c

    lax.fori_loop(1, n, send, 0)

    half = heads // 4 * 2
    per_head(0, half, head_dim, work)
    lane = lax.broadcasted_iota(jnp.int32, (rows, 128), 1) * head_dim
    index = lax.broadcasted_iota(jnp.int32, (rows, 128), 0) + me * rows
    mine = (index >= lane) & (index < lane + head_dim)

    def step(i, state):
        b = n - 1 - i if reverse else i

        @pl.when(b != me)
        def _():
            extra_copy(b, b).wait_recv()
            piece_copy(b, b).wait_recv()

        outbox[b] = state.astype(jnp.bfloat16)

        @pl.when(b != me)
        def _():
            result_copy(b, me).start()

        row = decays[b]
        factor = jnp.exp(jnp.sum(jnp.where(mine, row, 0.0), axis=1, keepdims=True))
        return factor * state + inbox[b].astype(jnp.float32)

    lax.fori_loop(0, n, step, jnp.zeros(inbox.shape[1:], jnp.float32))
    out[me] = outbox[me]
    per_head(half, heads, head_dim, work)

    def finish(k, c):
        peer = lax.rem(me + k, n)
        extra_copy(peer, peer).wait_send()
        piece_copy(peer, peer).wait_send()
        result_copy(peer, peer).wait_send()
        result_copy(peer, peer).wait_recv()
        return c

    lax.fori_loop(1, n, finish, 0)


def carried(flat, extra, decays, heads, depth, reverse, work, work_args, work_outs):
    n = lax.axis_size("seq")
    rows, width = flat.shape[0] // n, flat.shape[1]
    pieces = flat.reshape(n, rows, width)
    vmem = pl.BlockSpec(memory_space=pltpu.VMEM)
    args = (pieces, extra) + ((decays,) if reverse else ()) + tuple(work_args)
    out, gathered, *results = pl.pallas_call(
        functools.partial(scan_kernel, n, rows, heads, depth, reverse, work, len(work_args), len(work_outs)),
        out_shape=(
            jax.ShapeDtypeStruct((n, rows, width), jnp.bfloat16),
            jax.ShapeDtypeStruct((n,) + extra.shape, jnp.float32),
        ) + tuple(work_outs),
        in_specs=[vmem] * (len(args) - len(work_args)) + [pl.BlockSpec(memory_space=pltpu.SMEM)]
        + [vmem] * (len(work_args) - 1),
        out_specs=(vmem,) * (2 + len(work_outs)),
        scratch_shapes=[pltpu.VMEM((n, rows, width), jnp.bfloat16)] * 2
        + [pltpu.SemaphoreType.DMA((n,))] * 6,
        compiler_params=pltpu.CompilerParams(
            collective_id=1 if reverse else 0, has_side_effects=True, vmem_limit_bytes=48 << 20),
        name="adjoint_scan" if reverse else "state_scan",
    )(*args)
    return (out.reshape(n * rows, width), gathered, *results)


def tail_kernel(n, terms, edge, total, following, held, landed, send_sem, recv_sem, edge_send, edge_recv):
    me = lax.axis_index("seq")
    group = lax.axis_index("groups")
    steps = n.bit_length() - 1
    barrier = pltpu.get_barrier_semaphore()
    partners = [me + (1 << i) - (2 << i) * ((me // (1 << i)) % 2) for i in range(steps)]
    for partner in partners:
        pl.semaphore_signal(barrier, inc=1, device_id=(group, partner), device_id_type=MESH)
    before, after = lax.rem(me + n - 1, n), lax.rem(me + 1, n)
    for peer in (before, after):
        pl.semaphore_signal(barrier, inc=1, device_id=(group, peer), device_id_type=MESH)
    pl.semaphore_wait(barrier, steps + 2)
    edge_copy = pltpu.make_async_remote_copy(
        src_ref=edge, dst_ref=following, send_sem=edge_send, recv_sem=edge_recv,
        device_id=(group, before), device_id_type=MESH)
    edge_copy.start()
    held[0] = terms[...]
    for i, partner in enumerate(partners):
        copy = pltpu.make_async_remote_copy(
            src_ref=held.at[i], dst_ref=landed.at[i], send_sem=send_sem.at[i], recv_sem=recv_sem.at[i],
            device_id=(group, partner), device_id_type=MESH)
        copy.start()
        copy.wait()
        held[i + 1] = held[i] + landed[i]
    total[...] = held[steps]
    edge_copy.wait()


def tail_exchange(terms, edge):
    n = lax.axis_size("seq")
    steps = n.bit_length() - 1
    vmem = pl.BlockSpec(memory_space=pltpu.VMEM)
    return pl.pallas_call(
        functools.partial(tail_kernel, n),
        out_shape=(jax.ShapeDtypeStruct(terms.shape, jnp.float32), jax.ShapeDtypeStruct(edge.shape, jnp.float32)),
        in_specs=[vmem, vmem],
        out_specs=(vmem, vmem),
        scratch_shapes=[
            pltpu.VMEM((steps + 1,) + terms.shape, jnp.float32),
            pltpu.VMEM((steps,) + terms.shape, jnp.float32),
            pltpu.SemaphoreType.DMA((steps,)),
            pltpu.SemaphoreType.DMA((steps,)),
            pltpu.SemaphoreType.DMA,
            pltpu.SemaphoreType.DMA,
        ],
        compiler_params=pltpu.CompilerParams(collective_id=2, has_side_effects=True),
        name="tail_exchange",
    )(terms, edge)


def passed_along(value, axis):
    count = lax.axis_size(axis)
    return lax.ppermute(value, axis, [(s, s + 1) for s in range(count - 1)])


def mm(a, b, ca, cb):
    return lax.dot_general(a, b, (((ca,), (cb,)), ((), ())), preferred_element_type=jnp.float32)


def framed_outer(left, right, late, w0, w1):
    second = right * late
    first = right - second
    return (w0 * mm(left, first, 1, 1) + w1 * mm(left, second, 1, 1)).astype(jnp.bfloat16)


def per_head(start, stop, dim, work):
    def pair(i, carry):
        for j in range(2):
            h = i * 2 + j
            work(h, pl.ds(pl.multiple_of(h * dim, 16), dim))
        return carry

    lax.fori_loop(start // 2, stop // 2, pair, 0)
    if stop % 2:
        work(stop - 1, pl.ds((stop - 1) * dim, dim))


def heads_per_step(heads):
    return next(k for k in (4, 2, 1) if heads % k == 0)


def step_heads(heads, dim, work):
    count = heads_per_step(heads)
    for j in range(count):
        work(pl.program_id(0) * count + j, slice(j * dim, (j + 1) * dim))


def delayed(value, before, taps):
    count = value.shape[1]
    joined = jnp.concatenate([before, value], axis=1)
    width = joined.shape[1]
    return [value] + [pltpu.roll(joined, j, 1)[:, width - count :] for j in range(1, taps)]


def pre_kernel(heads, dim, tap_count, scal, late, key, value, before, columns, conv, state):
    def work(h, c):
        x = delayed(value[c, :].astype(jnp.float32), before[c, :].astype(jnp.float32), tap_count)
        cols = columns[c, :]
        total = cols[:, 0:1] * x[0]
        for j in range(1, tap_count):
            total = total + cols[:, j : j + 1] * x[j]
        v = total.astype(jnp.bfloat16)
        conv[c, :] = v
        state[c, :] = framed_outer(v, key[c, :], late[...], scal[0, h], 1.0)

    step_heads(heads, dim, work)


def ahead_work(scal, same, cross, query, key, conv, part, h, c):
    weight = same[...] + scal[0, h] * cross[...]
    attn = (mm(key[c, :], query[c, :], 0, 0) * weight).astype(jnp.bfloat16)
    part[c, :] = mm(conv[c, :], attn, 1, 0)


def back_work(scal, late, same, cross, query, key, conv, grad, state, grad_query, key_part, value_part, h, c):
    row_scale = jnp.where(late[0:1, :].astype(jnp.float32) > 0.5, scal[2, h], scal[1, h])
    q, k, g = query[c, :], key[c, :], grad[c, :]
    weight = same[...] + scal[0, h] * cross[...]
    attn = (mm(k, q, 0, 0) * weight).astype(jnp.bfloat16)
    score = (mm(conv[c, :], g, 0, 0) * weight).astype(jnp.bfloat16)
    grad_query[c, :] = (mm(k, score, 1, 0) + row_scale * mm(state[c, :], g, 0, 0)).astype(jnp.bfloat16)
    key_part[c, :] = mm(q, score, 1, 1)
    value_part[c, :] = mm(g, attn, 1, 1)


def mid_kernel(heads, dim, tap_count, scal, late, query, part, upstream, columns, state, grad, adjoint, terms):
    is_late = late[0:1, :].astype(jnp.float32) > 0.5

    def work(h, c):
        q = query[c, :]
        row_scale = jnp.where(is_late, scal[2, h], scal[1, h])
        numerator = part[c, :] + row_scale * mm(state[c, :], q, 1, 0)
        inv_rms = lax.rsqrt(jnp.mean(numerator * numerator, axis=0, keepdims=True) + EPSILON)
        normed = numerator * inv_rms
        up = upstream[c, :].astype(jnp.float32)
        terms[c, :] = jnp.sum(up * normed, axis=1, keepdims=True)
        normed_grad = up * columns[c, :][:, tap_count : tap_count + 1]
        g = (inv_rms * (
            normed_grad - normed * jnp.mean(normed_grad * normed, axis=0, keepdims=True)
        )).astype(jnp.bfloat16)
        grad[c, :] = g
        adjoint[c, :] = framed_outer(g, q, late[...], scal[1, h], scal[2, h])

    step_heads(heads, dim, work)


def post_kernel(heads, dim, tap_count, scal, late, key, conv, value, before, columns, adjoint, key_part,
                value_part, grad_key, grad_value, tap_terms, opening, ending):
    is_late = late[0:1, :].astype(jnp.float32) > 0.5

    def work(h, c):
        into_end = jnp.where(is_late, 1.0, scal[0, h])
        adj = adjoint[c, :]
        grad_key[c, :] = (key_part[c, :] + into_end * mm(adj, conv[c, :], 0, 0)).astype(jnp.bfloat16)
        own = value_part[c, :] + into_end * mm(adj, key[c, :], 1, 0)
        opening[c, :] = own[:, :128]
        count = own.shape[1]
        x = delayed(value[c, :].astype(jnp.float32), before[c, :].astype(jnp.float32), tap_count)
        joined = jnp.concatenate([own, jnp.zeros((dim, 128), jnp.float32)], axis=1)
        cols = columns[c, :]
        total = cols[:, 0:1] * own
        tap_terms[c, 0:1] = jnp.sum(own * x[0], axis=1, keepdims=True)
        for j in range(1, tap_count):
            total = total + cols[:, j : j + 1] * pltpu.roll(joined, count + 128 - j, 1)[:, :count]
            tap_terms[c, j : j + 1] = jnp.sum(own * x[j], axis=1, keepdims=True)
        grad_value[c, :] = total.astype(jnp.bfloat16)
        ending[c, :] = total[:, count - 128 :]

    step_heads(heads, dim, work)


def end_kernel(whole, tile, out):
    out[...] = tile[...].astype(jnp.bfloat16)


def local_call(kernel, name, heads, dim, args, outs):
    rows = heads_per_step(heads) * dim

    def spec(array):
        if array.shape[0] >= heads * dim:
            return pl.BlockSpec((rows, array.shape[1]), lambda i: (i, 0))
        return pl.BlockSpec(array.shape, lambda i: (0, 0))

    return pl.pallas_call(
        kernel,
        grid=(heads * dim // rows,),
        out_shape=tuple(outs),
        in_specs=[pl.BlockSpec(memory_space=pltpu.SMEM)] + [spec(a) for a in args[1:]],
        out_specs=tuple(spec(a) for a in outs),
        compiler_params=pltpu.CompilerParams(vmem_limit_bytes=40 << 20),
        name=name,
    )(*args)


def body(
    queries,
    key_rows,
    value_rows,
    frame_len,
    log_decay,
    timestep,
    conv_kernel,
    norm_gain,
    mod_table,
    out_grad,
):
    f32, bf16 = jnp.float32, jnp.bfloat16
    shape = jax.ShapeDtypeStruct
    row_count, channels = queries.shape
    head_count = log_decay.shape[2]
    head_dim = channels // head_count
    score_scale = head_dim ** (-0.5)
    tap_count = conv_kernel.shape[0]
    block_count = lax.axis_size("seq")
    place = lax.axis_index("seq")
    state_rows = -(-channels // (16 * block_count)) * 16 * block_count

    span = tap_count - 1
    previous = passed_along(value_rows[row_count - span :], "seq")
    before = jnp.pad(previous.T, ((0, 0), (128 - span, 0)))
    query_t, key_t, value_t, upstream_t = (a.T for a in (queries, key_rows, value_rows, out_grad))
    cum0 = log_decay[0, 0]
    cum1 = cum0 + log_decay[0, 1]
    scal = jnp.stack([jnp.exp(cum1 - cum0), score_scale * jnp.exp(cum0), score_scale * jnp.exp(cum1)])
    first = frame_len[0, 0]
    late_at = lambda size, axis: lax.broadcasted_iota(jnp.int32, size, axis) >= first
    late = late_at((head_dim, row_count), 1).astype(bf16)
    square = (row_count, row_count)
    late_s, late_t = late_at(square, 0), late_at(square, 1)
    same = jnp.where(late_t == late_s, score_scale, 0.0).astype(f32)
    cross = jnp.where(late_t & ~late_s, score_scale, 0.0).astype(f32)
    levels = jnp.arange(mod_table.shape[0], dtype=jnp.int32)
    mod_row = lax.dynamic_index_in_dim(mod_table, timestep[0], 0, True)
    gain = norm_gain[None, :] * (1.0 + mod_row)
    columns = jnp.concatenate([conv_kernel, gain], axis=0).T
    lanes = jnp.concatenate([
        cum1, timestep.astype(f32), jnp.zeros((128 - head_count - 1,), f32)])[None, :]

    sizes = (head_count, head_dim, tap_count)
    whole = (channels, row_count)
    conv_values, local_state = local_call(
        functools.partial(pre_kernel, *sizes), "conv_state", head_count, head_dim,
        (scal, late, key_t, value_t, before, columns),
        (shape(whole, bf16), shape((state_rows, head_dim), bf16)))
    state_in, gathered, part = carried(
        local_state, lanes, None, head_count, head_dim, False, ahead_work,
        (scal, same, cross, query_t, key_t, conv_values), (shape(whole, f32),))
    grad, adjoint_local, block_terms = local_call(
        functools.partial(mid_kernel, *sizes), "heads", head_count, head_dim,
        (scal, late, query_t, part, upstream_t, columns, state_in),
        (shape(whole, bf16), shape((state_rows, head_dim), bf16), shape((channels, 1), f32)))
    adjoint, terms_all, query_grad, key_part, value_part = carried(
        adjoint_local, block_terms.reshape(1, channels), gathered, head_count, head_dim, True, back_work,
        (scal, late, same, cross, query_t, key_t, conv_values, grad, state_in),
        (shape(whole, bf16), shape(whole, f32), shape(whole, f32)))
    key_grad, value_grad, tap_terms, opening, ending = local_call(
        functools.partial(post_kernel, *sizes), "adjoint_terms", head_count, head_dim,
        (scal, late, key_t, conv_values, value_t, before, columns, adjoint, key_part, value_part),
        (shape(whole, bf16), shape(whole, bf16), shape((channels, tap_count), f32),
         shape((channels, 128), f32), shape((channels, 128), f32)))
    kernel_sum, following = tail_exchange(tap_terms.T, opening[:, :span].T)
    following = jnp.where(place == block_count - 1, 0.0, following).T
    fixed = []
    for i in range(span):
        column = jnp.zeros((channels,), f32)
        for j in range(span - i, tap_count):
            column = column + conv_kernel[j] * following[:, i + j - span]
        fixed.append(column)
    tile = ending + jnp.pad(jnp.stack(fixed, axis=1), ((0, 0), (128 - span, 0)))
    value_grad = pl.pallas_call(
        end_kernel,
        grid=(1,),
        out_shape=shape(whole, bf16),
        in_specs=[pl.BlockSpec(memory_space=pl.ANY), pl.BlockSpec((channels, 128), lambda i: (0, 0))],
        out_specs=pl.BlockSpec((channels, 128), lambda i: (0, row_count // 128 - 1)),
        input_output_aliases={0: 0},
        name="last_tokens",
    )(value_grad, tile)
    query_grad, key_grad, value_grad = query_grad.T, key_grad.T, value_grad.T
    terms = terms_all[:, 0, :]
    chosen = (gathered[:, 0, head_count].astype(jnp.int32)[:, None] == levels[None, :]).astype(f32)
    sums = jnp.einsum("bl,bc->lc", chosen, terms, precision=lax.Precision.HIGHEST)
    gain_sum = jnp.sum(sums * (1.0 + mod_table), axis=0)
    table_sum = sums * norm_gain
    return (
        query_grad,
        key_grad,
        value_grad,
        kernel_sum / block_count,
        gain_sum / block_count,
        table_sum / block_count,
    )


def solution(mesh):
    in_specs = (
        P(("groups", "seq"), None),
        P(("groups", "seq"), None),
        P(("groups", "seq"), None),
        P(("groups", "seq"), None),
        P(("groups", "seq"), None, None),
        P(("groups", "seq")),
        P(),
        P(),
        P(),
        P(("groups", "seq"), None),
    )
    out_specs = (
        P(("groups", "seq"), None),
        P(("groups", "seq"), None),
        P(("groups", "seq"), None),
        P("groups", None),
        P("groups"),
        P("groups", None),
    )
    return jax.shard_map(body, mesh=mesh, in_specs=in_specs, out_specs=out_specs, check_vma=False)
```
